512 devices in a mesh: gx: 32 (over y, x), gy: 16 (over z, core).
Axes of the slice: x: 4, y: 8, z: 8, core: 2. Of those that a mesh axis runs over, the one named last changes fastest.
Arguments:
- source: float32 [256, 256, 512], P('gx', 'gy'), may hold values from -6 to 6
- face_coef: bfloat16 [3, 256, 256, 512], P(None, 'gx', 'gy'), may hold values from 0.25 to 4
Outputs:
- potential: float32 [256, 256, 512], P('gx', 'gy')
The draws below stay inside these ranges and needn't reach their ends.
All inputs are finite; a program needn't handle non-finite values.
Results may differ from the reference program's by a relative error of at most 0.0003.
Values sent between devices are 32-bit elements; how exact they have to be, the bound alone decides.
A program may use at most 64 MiB of HBM per device.

```python
import math
import jax
import jax.numpy as jnp

NZ = 512
LEVELS = 3
SWEEPS = 2
NX = 256
NY = 256


def draw_source(key, part):
    return jax.random.truncated_normal(key, -6.0, 6.0, (NX, NY, NZ), jnp.float32)


def shard_levels(key, shape, pieces, smallest, largest):
    loudness = 1.0
    for dim, blocks in pieces:
        heights = jax.random.uniform(jax.random.fold_in(jax.random.fold_in(key, 6), dim), (blocks,), jnp.float32, smallest / len(pieces), largest / len(pieces))
        loudness = loudness * jnp.repeat(jnp.exp(heights), shape[dim] // blocks).reshape((-1,) + (1,) * (len(shape) - 1 - dim))
    return loudness


def setup_inputs(seed: int = 0) -> dict:
    key_list = jax.random.split(jax.random.key(seed), 3)
    source = draw_source(jax.random.fold_in(key_list[2], 71), 0)
    face_coef = jnp.clip(jnp.exp(math.log(4.0) - 2.7725887 * jax.random.uniform(key_list[1], (3, NX, NY, NZ), jnp.float32) ** shard_levels(key_list[1], (3, NX, NY, NZ), ((1, 32), (2, 16)), -0.2, 0.2)), 0.25, 4.0).astype(jnp.bfloat16)
    return {"source": source, "face_coef": face_coef}


MASS = 0.002


def coarsen(couplings):
    east_face = couplings[0][1::2]
    east_face = east_face[:, 0::2, 0::2] + east_face[:, 1::2, 0::2] + east_face[:, 0::2, 1::2] + east_face[:, 1::2, 1::2]
    north_face = couplings[1][:, 1::2]
    north_face = north_face[0::2, :, 0::2] + north_face[1::2, :, 0::2] + north_face[0::2, :, 1::2] + north_face[1::2, :, 1::2]
    upper_face = couplings[2][:, :, 1::2]
    upper_face = upper_face[0::2, 0::2] + upper_face[1::2, 0::2] + upper_face[0::2, 1::2] + upper_face[1::2, 1::2]
    return jnp.stack((east_face, north_face, upper_face)) * 0.0625


def restrict(residual):
    dims = residual.shape
    return residual.reshape(dims[0] // 2, 2, dims[1] // 2, 2, dims[2] // 2, 2).mean(axis=(1, 3, 5))


def prolong(correction):
    return jnp.repeat(jnp.repeat(jnp.repeat(correction, 2, 0), 2, 1), 2, 2)


def neighbour_sum(potential, couplings, lagged):
    summed = couplings[0] * jnp.roll(potential, -1, 0) + lagged[0] * jnp.roll(potential, 1, 0)
    summed = summed + couplings[1] * jnp.roll(potential, -1, 1) + lagged[1] * jnp.roll(potential, 1, 1)
    summed = summed + couplings[2] * jnp.roll(potential, -1, 2) + lagged[2] * jnp.roll(potential, 1, 2)
    return summed


def parity_of(dims):
    row_ids = jnp.arange(dims[0], dtype=jnp.int32)
    col_ids = jnp.arange(dims[1], dtype=jnp.int32)
    depth_ids = jnp.arange(dims[2], dtype=jnp.int32)
    return (row_ids[:, None, None] + col_ids[None, :, None] + depth_ids[None, None, :]) % 2


def smoothing(potential, right_side, couplings, lagged, diagonal, parity):
    for sweep_index in range(SWEEPS):
        for colour in (0, 1):
            updated = (right_side + neighbour_sum(potential, couplings, lagged)) / diagonal
            potential = jnp.where(parity == colour, updated, potential)
    return potential


def coarse_solve(right_side, couplings):
    averages = jnp.mean(couplings, axis=(1, 2, 3))
    dims = right_side.shape
    eigen_parts = []
    for axis_index in range(3):
        wave = jnp.arange(dims[axis_index], dtype=jnp.int32).astype(jnp.float32) * (2.0 * math.pi / dims[axis_index])
        eigen_parts.append(2.0 * averages[axis_index] * (1.0 - jnp.cos(wave)))
    eigenvalue = MASS + eigen_parts[0][:, None, None] + eigen_parts[1][None, :, None] + eigen_parts[2][None, None, :]
    spectrum = jnp.fft.fftn(right_side) / eigenvalue
    return jnp.real(jnp.fft.ifftn(spectrum)).astype(right_side.dtype)


def multigrid_cycle(right_side, couplings, level_index):
    if level_index == LEVELS - 1:
        return coarse_solve(right_side, couplings)
    lagged = [jnp.roll(couplings[axis_index], 1, axis_index) for axis_index in range(3)]
    diagonal = MASS + couplings[0] + lagged[0] + couplings[1] + lagged[1] + couplings[2] + lagged[2]
    parity = parity_of(right_side.shape)
    potential = smoothing(jnp.zeros_like(right_side), right_side, couplings, lagged, diagonal, parity)
    residual = right_side - (diagonal * potential - neighbour_sum(potential, couplings, lagged))
    correction = multigrid_cycle(restrict(residual), coarsen(couplings), level_index + 1)
    potential = potential + prolong(correction)
    return smoothing(potential, right_side, couplings, lagged, diagonal, parity)


def reference(source, face_coef):
    return multigrid_cycle(source, face_coef.astype(jnp.float32), 0)
```

```python
import functools

import jax
import jax.numpy as jnp
import numpy as np
from jax import lax
from jax.experimental import pallas as pl
from jax.experimental.pallas import tpu as pltpu
from jax.sharding import PartitionSpec as P

MASS = 0.002
LX, LY = 8, 16
LANES = 128
MESH = pl.DeviceIdType.MESH
F32 = jnp.float32


def cas(rows, cols, length):
    angle = 2.0 * np.pi * ((rows * cols) % length) / length
    return np.cos(angle) + np.sin(angle)


@functools.lru_cache(maxsize=4)
def tables(gxn, gyn):
    nx, ny = 2 * gxn, 4 * gyn
    lanes = np.arange(LANES)
    depth = cas(lanes[:, None], lanes[None, :], LANES)
    rows = np.arange(nx)
    along_x = np.kron(cas(rows[:, None], rows[None, :], nx), np.eye(4))
    padded = along_x[(np.arange(4 * nx + 16) - 8) % (4 * nx)]
    cols = np.arange(ny)
    first = np.zeros((gyn, 2, 4, gyn, 2, 4))
    last = np.zeros((gyn, 6, 8, gyn, 6, 4))
    for me in range(gyn):
        table = cas((4 * me + np.arange(4))[:, None], cols[None, :], ny).reshape(4, gyn, 4)
        for i in range(2):
            first[me, i, :, :, i, :] = table
        table = cas(((4 * me - 2 + np.arange(8)) % ny)[:, None], cols[None, :], ny).reshape(8, gyn, 4)
        for i in range(6):
            last[me, i, :, :, i, :] = table
    first = first.reshape(gyn, 8, gyn * 8)
    last = last.reshape(gyn, 48, gyn * 24)
    wave_x = np.repeat(2.0 - 2.0 * np.cos(2.0 * np.pi * rows / nx), 4)[:, None] * np.ones((1, LANES))
    ky = 4 * np.arange(gyn)[:, None] + np.tile(np.arange(4), 2)[None, :]
    wave_y = (2.0 - 2.0 * np.cos(2.0 * np.pi * ky / ny))[:, :, None] * np.ones((1, 1, LANES))
    wave_z = (2.0 - 2.0 * np.cos(2.0 * np.pi * lanes / LANES))[None, :] * np.ones((8, 1))
    pick = np.zeros((4 * LANES, 4 * LANES))
    column = np.arange(4 * LANES)
    pick[4 * (column % LANES) + column // LANES, column] = 1.0
    out = [np.asarray(t, np.float32) for t in (depth, padded, first, last, wave_x, wave_y, wave_z)]
    return out + [pick.astype(jnp.bfloat16)]


def permuted(values, pick, dims):
    total = None
    rest = values
    for _ in range(3):
        part = rest.astype(jnp.bfloat16)
        rest = rest - part.astype(F32)
        term = lax.dot_general(part, pick, (dims, ((), ())), preferred_element_type=F32)
        total = term if total is None else total + term
    return total


def dot(a, b):
    return lax.dot_general(
        a, b, (((1,), (0,)), ((), ())), precision=lax.Precision.HIGHEST, preferred_element_type=F32
    )


def kernel(
    gxn,
    gyn,
    src_ref,
    coef_ref,
    depth_ref,
    alongx_ref,
    first_ref,
    last_ref,
    wavex_ref,
    wavey_ref,
    wavez_ref,
    pick_ref,
    out_ref,
    W,
    V,
    C,
    G,
    DG,
    T,
    W1,
    D1,
    I1,
    C1,
    B1,
    V1,
    VB,
    T1,
    Z,
    G1,
    G2,
    G3,
    DI,
    S1,
    S2,
    CR,
    Q,
    M3,
    face_s,
    face_r,
    blk_s,
    blk_r,
    g1_s,
    g1_r,
    g2_s,
    g2_r,
    g3_s,
    g3_r,
    c1_s,
    c1_r,
    c2_s,
    c2_r,
    m_sem,
):
    gx = lax.axis_index("gx")
    gy = lax.axis_index("gy")

    def at(dx, dy):
        return (lax.rem(gx + dx + gxn, gxn), lax.rem(gy + dy + gyn, gyn))

    around = [(dx, dy) for dx in (-1, 0, 1) for dy in (-1, 0, 1) if (dx, dy) != (0, 0)]

    barrier = pltpu.get_barrier_semaphore()
    for dx, dy in around:
        if dx and dy:
            pl.semaphore_signal(barrier, inc=1, device_id=at(dx, dy), device_id_type=MESH)

    def greet_x(i, carry):
        pl.semaphore_signal(barrier, inc=1, device_id=(lax.rem(gx + 1 + i, gxn), gy), device_id_type=MESH)
        return carry

    def greet_y(i, carry):
        pl.semaphore_signal(barrier, inc=1, device_id=(gx, lax.rem(gy + 1 + i, gyn)), device_id_type=MESH)
        return carry

    lax.fori_loop(0, gxn - 1, greet_x, 0)
    lax.fori_loop(0, gyn - 1, greet_y, 0)

    m3_copy = pltpu.make_async_copy(last_ref.at[gy], M3, m_sem)
    m3_copy.start()

    def remote(src, dst, ssem, rsem, dev):
        return pltpu.make_async_remote_copy(
            src_ref=src, dst_ref=dst, send_sem=ssem, recv_sem=rsem, device_id=dev, device_id_type=MESH
        )

    def start(copies):
        for copy in copies:
            copy.start()

    def wait(copies):
        for copy in copies:
            copy.wait()

    def faces(c, k):
        own = pl.ds(8, 2 * LY)
        ends = (
            (V.at[c, LX, own], V.at[c, 0, own], (1, 0)),
            (V.at[c, 1, own], V.at[c, LX + 1, own], (-1, 0)),
            (V.at[c, pl.ds(1, LX), pl.ds(32, 8)], V.at[c, pl.ds(1, LX), pl.ds(0, 8)], (0, 1)),
            (V.at[c, pl.ds(1, LX), pl.ds(8, 8)], V.at[c, pl.ds(1, LX), pl.ds(40, 8)], (0, -1)),
        )
        return [remote(s, d, face_s.at[k, i], face_r.at[k, i], at(*to)) for i, (s, d, to) in enumerate(ends)]

    def blocks(src, dst, k):
        copies = []
        for i, (dx, dy) in enumerate(around):
            there = dst.at[:, pl.ds(4 - 4 * dx, 4), pl.ds(16 - 8 * dy, 8)]
            copies.append(
                remote(src.at[:, pl.ds(4, 4), pl.ds(16, 8)], there, blk_s.at[k, i], blk_r.at[k, i], at(dx, dy))
            )
        return copies

    def gather(ref, along_gx, ssem, rsem):
        me, count = (gx, gxn) if along_gx else (gy, gyn)

        def peer(i):
            return lax.rem(me + 1 + i, count)

        def send(i, carry):
            dev = (peer(i), gy) if along_gx else (gx, peer(i))
            remote(ref.at[me], ref.at[me], ssem.at[i], rsem.at[me], dev).start()
            return carry

        def finish():
            def take(i, carry):
                dev = (peer(i), gy) if along_gx else (gx, peer(i))
                copy = remote(ref.at[me], ref.at[peer(i)], ssem.at[i], rsem.at[peer(i)], dev)
                copy.wait_send()
                copy.wait_recv()
                return carry

            lax.fori_loop(0, count - 1, take, 0)

        lax.fori_loop(0, count - 1, send, 0)
        return finish

    def iota(shape, dim):
        return lax.broadcasted_iota(jnp.int32, shape, dim)

    def spread(values, x, put):
        even = ((iota((LY, LANES), 0) + x) & 1) == 0
        for h in (0, 1):
            a = values[:, 2 * h * LANES : (2 * h + 1) * LANES]
            b = values[:, (2 * h + 1) * LANES : (2 * h + 2) * LANES]
            put(0, h, jnp.where(even, a, b))
            put(1, h, jnp.where(even, b, a))

    for d in range(3):
        flat = coef_ref[d].reshape(LX * LY, 4 * LANES)
        mixed = lax.dot_general(flat, pick_ref[...], (((1,), (0,)), ((), ())), preferred_element_type=F32)
        for x in range(LX):

            def put(c, h, values, d=d, x=x):
                W[2 * d + c, x + 1, pl.ds(8 + h, LY, stride=2), :] = values

            spread(mixed[x * LY : (x + 1) * LY], x, put)

    pl.semaphore_wait(barrier, gxn - 1 + gyn - 1 + 4)

    back = [
        remote(
            W.at[pl.ds(0, 2), LX, pl.ds(8, 2 * LY)],
            W.at[pl.ds(0, 2), 0, pl.ds(8, 2 * LY)],
            face_s.at[8, 0],
            face_r.at[8, 0],
            at(1, 0),
        ),
        remote(
            W.at[pl.ds(2, 2), pl.ds(1, LX), pl.ds(32, 8)],
            W.at[pl.ds(2, 2), pl.ds(1, LX), pl.ds(0, 8)],
            face_s.at[8, 1],
            face_r.at[8, 1],
            at(0, 1),
        ),
    ]
    start(back)

    mixed = permuted(src_ref[...].reshape(LX * LY, 4 * LANES), pick_ref[...], ((1,), (0,)))
    for x in range(LX):

        def put(c, h, values, x=x):
            G[c, x, pl.ds(h, LY, stride=2), :] = values

        spread(mixed[x * LY : (x + 1) * LY], x, put)

    own = pl.ds(8, 2 * LY)
    s32 = iota((2 * LY, LANES), 0)
    h_zero = (s32 & 1) == 0
    y_par = (s32 >> 1) & 1
    j8 = iota((8, LANES), 0)

    def pairs(i, values):
        T[i] = values
        return [T[i, pl.ds(h, 8, stride=4), :] + T[i, pl.ds(h + 2, 8, stride=4), :] for h in (0, 1)]

    def colours(i, two, scale):
        even = ((j8 + i) & 1) == 0
        return jnp.where(even, two[0], two[1]) * scale, jnp.where(even, two[1], two[0]) * scale

    def coarsen(i, carry):
        lo, hi = 1 + 2 * i, 2 + 2 * i
        mine = pl.ds(16, 8)
        e, o = colours(i, pairs(i, W[0, hi, own] + W[1, hi, own]), 0.0625)
        W1[0, 4 + i, mine] = e
        W1[1, 4 + i, mine] = o
        T[i] = W[2, lo, own] + W[3, lo, own] + W[2, hi, own] + W[3, hi, own]
        e, o = colours(i, [T[i, pl.ds(2 + h, 8, stride=4), :] for h in (0, 1)], 0.0625)
        W1[2, 4 + i, mine] = e
        W1[3, 4 + i, mine] = o
        even = y_par == 0
        low = jnp.where(even, W[5, lo, own], W[4, lo, own])
        e, o = colours(i, pairs(i, low + jnp.where(even, W[4, hi, own], W[5, hi, own])), 0.0625)
        W1[4, 4 + i, mine] = e
        W1[5, 4 + i, mine] = o
        return carry

    lax.fori_loop(0, 4, coarsen, 0)
    w1_copies = blocks(W1, W1, 0)

    def other(read, c, parity):
        pc0 = y_par == (parity ^ c)
        up, down = read(1), read(-1)
        return jnp.where(
            h_zero,
            jnp.where(pc0, pltpu.roll(up, 1, 1), up),
            jnp.where(pc0, down, pltpu.roll(down, LANES - 1, 1)),
        )

    def coefficients(i, carry):
        for parity in (0, 1):
            x = 2 * i + parity
            for c in (0, 1):
                o = 1 - c
                pc0 = y_par == (parity ^ c)
                xp, xm = W[c, x + 1, own], W[o, x, own]
                yp, ym = W[2 + c, x + 1, own], W[2 + o, x + 1, pl.ds(6, 2 * LY)]
                zc, zo = W[4 + c, x + 1, own], W[4 + o, x + 1, own]
                zs = jnp.where(pc0, zc, zo)
                far = other(lambda ds: W[4 + o, x + 1, pl.ds(8 + ds, 2 * LY)], c, parity)
                zt = jnp.where(pc0, far, zc)
                diagonal = MASS + xp + xm + yp + ym + zs + zt
                inverse = 1.0 / diagonal
                for k, value in enumerate((xp, xm, yp, ym, zs, zt)):
                    C[c, k, x] = value * inverse
                DG[c, x] = diagonal
                G[c, x] = G[c, x] * inverse
                if c == 0:
                    V[0, x + 1, own] = G[0, x]
        return carry

    def weighted(c, x, parity):
        o = 1 - c
        total = G[c, x] + C[c, 0, x] * V[o, x + 2, own] + C[c, 1, x] * V[o, x, own]
        total = total + C[c, 2, x] * V[o, x + 1, pl.ds(10, 2 * LY)] + C[c, 3, x] * V[o, x + 1, pl.ds(6, 2 * LY)]
        far = other(lambda ds: V[o, x + 1, pl.ds(8 + ds, 2 * LY)], c, parity)
        return total + C[c, 4, x] * V[o, x + 1, own] + C[c, 5, x] * far

    def half_sweep(c):
        def rows(i, carry):
            for parity in (0, 1):
                x = 2 * i + parity
                V[c, x + 1, own] = weighted(c, x, parity)
            return carry

        lax.fori_loop(0, LX // 2, rows, 0)

    wait(back)
    lax.fori_loop(0, LX // 2, coefficients, 0)
    copies = faces(0, 0)
    start(copies)
    start(w1_copies)

    sums = []
    mine = pl.ds(16, 8)
    sums.append(W1[0, 5, mine] + W1[1, 5, mine] + W1[0, 7, mine] + W1[1, 7, mine])
    part_y, part_z = 0.0, 0.0
    for i in range(4):
        part_y = part_y + jnp.where((j8 & 1) == 1, W1[2, 4 + i, mine] + W1[3, 4 + i, mine], 0.0)
        part_z = part_z + jnp.where(((j8 + i) & 1) == 0, W1[5, 4 + i, mine], W1[4, 4 + i, mine])
    sums += [part_y, part_z]
    scale = 1.0 / (16.0 * 2 * gxn * 4 * gyn * LANES)
    lane = iota((1, LANES), 1)
    row = jnp.zeros((1, LANES), F32)
    for d in range(3):
        value = jnp.sum(jnp.sum(sums[d], axis=0, keepdims=True), axis=1, keepdims=True)
        row = row + jnp.where(lane == d, value * scale, 0.0)
    S1[gy] = row
    wait_c1 = gather(S1, False, c1_s, c1_r)

    wait(copies)
    half_sweep(1)
    copies = faces(1, 1)
    start(copies)

    wait(w1_copies)

    def z_terms(c, x, sub, parity_iota):
        o = 1 - c
        pc0 = ((parity_iota + x + c) & 1) == 0
        zc, zo = W1[4 + c, x, sub], W1[4 + o, x, sub]
        return jnp.where(pc0, zc, zo), jnp.where(pc0, pltpu.roll(zo, 1, 1), zc)

    def diagonals(i, carry):
        x = 4 + i
        for c in (0, 1):
            o = 1 - c
            zs, zt = z_terms(c, x, pl.ds(16, 8), j8)
            total = MASS + W1[c, x, pl.ds(16, 8)] + W1[o, x - 1, pl.ds(16, 8)]
            total = total + W1[2 + c, x, pl.ds(16, 8)] + W1[2 + o, x, pl.ds(15, 8)]
            D1[c, x, pl.ds(16, 8)] = total + zs + zt
        return carry

    lax.fori_loop(0, 4, diagonals, 0)
    d1_copies = blocks(D1, D1, 1)
    start(d1_copies)

    wait(copies)
    half_sweep(0)
    copies = faces(0, 2)
    start(copies)

    wait_c1()
    S2[gx] = jnp.sum(S1[...], axis=0)
    wait_c2 = gather(S2, True, c2_s, c2_r)

    wait(copies)
    half_sweep(1)
    copies = faces(1, 3)
    start(copies)

    wait(d1_copies)
    wide = pl.ds(8, 24)
    s24 = iota((24, LANES), 0)

    def inverses(x, carry):
        for c in (0, 1):
            I1[c, x] = 1.0 / D1[c, x, wide]
        return carry

    lax.fori_loop(0, 12, inverses, 0)

    def coefficients1(i, carry):
        x = 1 + i
        for c in (0, 1):
            o = 1 - c
            inverse = I1[c, x]
            zs, zt = z_terms(c, x, wide, s24)
            values = (W1[c, x, wide], W1[o, x - 1, wide], W1[2 + c, x, wide], W1[2 + o, x, pl.ds(7, 24)], zs, zt)
            for k, value in enumerate(values):
                C1[c, k, x] = value * inverse
        return carry

    lax.fori_loop(0, 10, coefficients1, 0)

    wait(copies)

    def restrict(i, carry):
        total = None
        for parity in (0, 1):
            x = 2 * i + parity
            for c in (0, 1):
                r = DG[c, x] * (weighted(c, x, parity) - V[c, x + 1, own])
                total = r if total is None else total + r
        e, o = colours(i, pairs(i, total), 0.125)
        B1[0, 4 + i, pl.ds(16, 8)] = e
        B1[1, 4 + i, pl.ds(16, 8)] = o
        return carry

    lax.fori_loop(0, 4, restrict, 0)
    copies = blocks(B1, B1, 2)
    start(copies)

    wait_c2()
    CR[...] = jnp.sum(S2[...], axis=0)
    mean = [jnp.sum(jnp.where(lane == d, CR[...], 0.0), axis=1, keepdims=True) for d in range(3)]
    cells = float(2 * gxn * 4 * gyn * LANES)
    flat_part = MASS + mean[1] * wavey_ref[gy] + mean[2] * wavez_ref[...]

    def eigen(i, carry):
        tile = pl.ds(pl.multiple_of(8 * i, 8), 8)
        DI[tile, :] = 1.0 / ((flat_part + mean[0] * wavex_ref[tile, :]) * cells)
        return carry

    lax.fori_loop(0, gxn, eigen, 0)

    def weighted1(A, c, x):
        o = 1 - c
        pc0 = ((s24 + x + c) & 1) == 0
        here = A[o, x, wide]
        total = B1[c, x, wide] * I1[c, x] + C1[c, 0, x] * A[o, x + 1, wide] + C1[c, 1, x] * A[o, x - 1, wide]
        total = total + C1[c, 2, x] * A[o, x, pl.ds(9, 24)] + C1[c, 3, x] * A[o, x, pl.ds(7, 24)]
        far = jnp.where(pc0, pltpu.roll(here, 1, 1), pltpu.roll(here, LANES - 1, 1))
        return total + C1[c, 4, x] * here + C1[c, 5, x] * far

    def half_sweep1(A, c, low):
        def rows(i, carry):
            x = low + i
            A[c, x, wide] = weighted1(A, c, x)
            return carry

        lax.fori_loop(0, 12 - 2 * low, rows, 0)

    wait(copies)

    def first1(x, carry):
        V1[0, x, wide] = B1[0, x, wide] * I1[0, x]
        return carry

    lax.fori_loop(0, 12, first1, 0)
    half_sweep1(V1, 1, 1)
    half_sweep1(V1, 0, 2)
    half_sweep1(V1, 1, 3)

    for i in range(2):
        total = None
        for k in range(2):
            x = 4 + 2 * i + k
            for c in (0, 1):
                r = (weighted1(V1, c, x) - V1[c, x, wide])[8:16] * D1[c, x, pl.ds(16, 8)]
                total = r if total is None else total + r
        T1[pl.ds(8, 8), :] = total
        Z[pl.ds(4 * i, 4), :] = (T1[pl.ds(8, 4, stride=2), :] + T1[pl.ds(9, 4, stride=2), :]) * 0.125

    G1[gy] = dot(Z[...], depth_ref[...])
    finish = gather(G1, False, g1_s, g1_r)
    v1_copies = blocks(V1, VB, 3)
    start(v1_copies)
    VB[:, pl.ds(4, 4), pl.ds(16, 8)] = V1[:, pl.ds(4, 4), pl.ds(16, 8)]
    finish()
    G2[gx] = dot(first_ref[gy], G1[...].reshape(8 * gyn, LANES))
    finish = gather(G2, True, g2_s, g2_r)
    finish()
    spectrum = dot(alongx_ref[pl.ds(8, 8 * gxn), :], G2[...].reshape(8 * gxn, LANES)) * DI[...]
    back_x = dot(alongx_ref[pl.ds(pl.multiple_of(8 * gx, 8), 24), :], spectrum)
    G3[gy] = dot(back_x, depth_ref[...])
    finish = gather(G3, False, g3_s, g3_r)
    m3_copy.wait()
    wait(v1_copies)
    finish()
    coarse = dot(M3[...], G3[...].reshape(24 * gyn, LANES))

    for a in range(6):
        part = coarse[8 * a : 8 * a + 8]
        T1[pl.ds(4, 8, stride=2), :] = part
        T1[pl.ds(5, 8, stride=2), :] = part
        for x in (2 * a, 2 * a + 1):
            for c in (0, 1):
                VB[c, x, wide] = VB[c, x, wide] + T1[...]
    half_sweep1(VB, 0, 1)
    half_sweep1(VB, 1, 2)
    half_sweep1(VB, 0, 3)
    half_sweep1(VB, 1, 4)

    def prolong(i, carry):
        even = ((j8 + i) & 1) == 0
        e, o = VB[0, 4 + i, pl.ds(16, 8)], VB[1, 4 + i, pl.ds(16, 8)]
        for h, part in enumerate((jnp.where(even, e, o), jnp.where(even, o, e))):
            T[i, pl.ds(h, 8, stride=4), :] = part
            T[i, pl.ds(h + 2, 8, stride=4), :] = part
        for x in (2 * i, 2 * i + 1):
            for c in (0, 1):
                V[c, x + 1, own] = V[c, x + 1, own] + T[i]
        return carry

    lax.fori_loop(0, 4, prolong, 0)
    for k, c in enumerate((1, 0, 1, 0)):
        copies = faces(c, 4 + k)
        start(copies)
        wait(copies)
        half_sweep(1 - c)

    for x in range(LX):
        even = ((iota((LY, LANES), 0) + x) & 1) == 0
        for h in (0, 1):
            e, o = V[0, x + 1, pl.ds(8 + h, LY, stride=2), :], V[1, x + 1, pl.ds(8 + h, LY, stride=2), :]
            rows = pl.ds(x * LY, LY)
            Q[rows, pl.ds(2 * h * LANES, LANES)] = jnp.where(even, e, o)
            Q[rows, pl.ds((2 * h + 1) * LANES, LANES)] = jnp.where(even, o, e)
    out_ref[...] = permuted(Q[...], pick_ref[...], ((1,), (1,))).reshape(LX, LY, 4 * LANES)


def solution(mesh):
    gxn, gyn = mesh.shape["gx"], mesh.shape["gy"]
    consts = tables(gxn, gyn)

    def step(source, face_coef):
        vmem = pl.BlockSpec(memory_space=pltpu.VMEM)
        dma = pltpu.SemaphoreType.DMA
        V = pltpu.VMEM
        return pl.pallas_call(
            functools.partial(kernel, gxn, gyn),
            out_shape=jax.ShapeDtypeStruct((LX, LY, 4 * LANES), F32),
            in_specs=[vmem] * 5 + [pl.BlockSpec(memory_space=pl.ANY)] + [vmem] * 4,
            out_specs=vmem,
            scratch_shapes=[
                V((6, LX + 2, 48, LANES), F32),
                V((2, LX + 2, 48, LANES), F32),
                V((2, 6, LX, 32, LANES), F32),
                V((2, LX, 32, LANES), F32),
                V((2, LX, 32, LANES), F32),
                V((4, 32, LANES), F32),
                V((6, 12, 40, LANES), F32),
                V((2, 12, 40, LANES), F32),
                V((2, 12, 24, LANES), F32),
                V((2, 6, 12, 24, LANES), F32),
                V((2, 12, 40, LANES), F32),
                V((2, 12, 40, LANES), F32),
                V((2, 12, 40, LANES), F32),
                V((24, LANES), F32),
                V((8, LANES), F32),
                V((gyn, 8, LANES), F32),
                V((gxn, 8, LANES), F32),
                V((gyn, 24, LANES), F32),
                V((8 * gxn, LANES), F32),
                V((gyn, 1, LANES), F32),
                V((gxn, 1, LANES), F32),
                V((1, LANES), F32),
                V((LX * LY, 4 * LANES), F32),
                V((48, 24 * gyn), F32),
                dma((9, 4)),
                dma((9, 4)),
                dma((4, 8)),
                dma((4, 8)),
                dma((gyn,)),
                dma((gyn,)),
                dma((gxn,)),
                dma((gxn,)),
                dma((gyn,)),
                dma((gyn,)),
                dma((gyn,)),
                dma((gyn,)),
                dma((gxn,)),
                dma((gxn,)),
                dma,
            ],
            compiler_params=pltpu.CompilerParams(
                collective_id=0, has_side_effects=True, vmem_limit_bytes=60 * 1024 * 1024
            ),
            name="cycle",
        )(source, face_coef, *[jnp.asarray(t) for t in consts])

    return jax.shard_map(
        step,
        mesh=mesh,
        in_specs=(P("gx", "gy", None), P(None, "gx", "gy", None)),
        out_specs=P("gx", "gy", None),
        check_vma=False,
    )
```

```python
import functools

import jax
import jax.numpy as jnp
import numpy as np
from jax import lax
from jax.experimental import pallas as pl
from jax.experimental.pallas import tpu as pltpu
from jax.sharding import PartitionSpec as P

MASS = 0.002
LX, LY = 8, 16
LANES = 128
MESH = pl.DeviceIdType.MESH
F32 = jnp.float32


def cas(rows, cols, length):
    angle = 2.0 * np.pi * ((rows * cols) % length) / length
    return np.cos(angle) + np.sin(angle)


@functools.lru_cache(maxsize=4)
def tables(gxn, gyn):
    nx, ny = 2 * gxn, 4 * gyn
    lanes = np.arange(LANES)
    depth = cas(lanes[:, None], lanes[None, :], LANES)
    rows = np.arange(nx)
    along_x = np.kron(cas(rows[:, None], rows[None, :], nx), np.eye(4))
    padded = along_x[(np.arange(4 * nx + 24) - 12) % (4 * nx)]
    cols = np.arange(ny)
    first = np.zeros((gyn, 2, 4, gyn, 2, 4))
    last = np.zeros((gyn, 16, gyn, 8, 4))
    for me in range(gyn):
        table = cas((4 * me + np.arange(4))[:, None], cols[None, :], ny).reshape(4, gyn, 4)
        for i in range(2):
            first[me, i, :, :, i, :] = table
        table = cas(((4 * me - 3 + np.arange(16)) % ny)[:, None], cols[None, :], ny).reshape(16, gyn, 4)
        last[me] = table[:, :, None, :]
    first = first.reshape(gyn, 8, gyn * 8)
    last = last.reshape(gyn, 16, gyn * 32)
    wave_x = np.repeat(2.0 - 2.0 * np.cos(2.0 * np.pi * rows / nx), 4)[:, None] * np.ones((1, LANES))
    ky = 4 * np.arange(gyn)[:, None] + np.tile(np.arange(4), 2)[None, :]
    wave_y = (2.0 - 2.0 * np.cos(2.0 * np.pi * ky / ny))[:, :, None] * np.ones((1, 1, LANES))
    wave_z = (2.0 - 2.0 * np.cos(2.0 * np.pi * lanes / LANES))[None, :] * np.ones((8, 1))
    pick = np.zeros((4 * LANES, 4 * LANES))
    column = np.arange(4 * LANES)
    pick[4 * (column % LANES) + column // LANES, column] = 1.0
    out = [np.asarray(t, np.float32) for t in (depth, along_x, padded, first, last, wave_x, wave_y, wave_z)]
    return out + [pick.astype(jnp.bfloat16)]


def permuted(values, pick, dims):
    total = None
    rest = values
    for _ in range(3):
        part = rest.astype(jnp.bfloat16)
        rest = rest - part.astype(F32)
        term = lax.dot_general(part, pick, (dims, ((), ())), preferred_element_type=F32)
        total = term if total is None else total + term
    return total


def dot(a, b):
    return lax.dot_general(
        a, b, (((1,), (0,)), ((), ())), precision=lax.Precision.HIGHEST, preferred_element_type=F32
    )


def kernel(
    gxn,
    gyn,
    src_ref,
    coef_ref,
    depth_ref,
    alongx_ref,
    padx_ref,
    first_ref,
    last_ref,
    wavex_ref,
    wavey_ref,
    wavez_ref,
    pick_ref,
    out_ref,
    WB,
    V,
    VQ,
    VP,
    C,
    G,
    DG,
    T,
    W1,
    D1,
    I1,
    C1,
    B1,
    V1,
    VB,
    T1,
    Z,
    G1,
    G2,
    G3,
    DI,
    S1,
    S2,
    CR,
    Q,
    LT,
    M3,
    l0_s,
    l0_r,
    blk_s,
    blk_r,
    g1_s,
    g1_r,
    g2_s,
    g2_r,
    g3_s,
    g3_r,
    c1_s,
    c1_r,
    c2_s,
    c2_r,
    m_sem,
):
    gx = lax.axis_index("gx")
    gy = lax.axis_index("gy")

    def at(dx, dy):
        return (lax.rem(gx + dx + gxn, gxn), lax.rem(gy + dy + gyn, gyn))

    corners = [(dx, dy) for dx in (1, -1) for dy in (1, -1)]
    around = [(1, 0), (-1, 0), (0, 1), (0, -1)] + corners

    barrier = pltpu.get_barrier_semaphore()
    for dx, dy in corners:
        for far in (1, 2):
            pl.semaphore_signal(barrier, inc=1, device_id=at(far * dx, dy), device_id_type=MESH)

    def greet_x(i, carry):
        pl.semaphore_signal(barrier, inc=1, device_id=(lax.rem(gx + 1 + i, gxn), gy), device_id_type=MESH)
        return carry

    def greet_y(i, carry):
        pl.semaphore_signal(barrier, inc=1, device_id=(gx, lax.rem(gy + 1 + i, gyn)), device_id_type=MESH)
        return carry

    lax.fori_loop(0, gxn - 1, greet_x, 0)
    lax.fori_loop(0, gyn - 1, greet_y, 0)

    table_copy = pltpu.make_async_copy(last_ref.at[gy], LT, m_sem)
    table_copy.start()

    def remote(src, dst, ssem, rsem, dev):
        return pltpu.make_async_remote_copy(
            src_ref=src, dst_ref=dst, send_sem=ssem, recv_sem=rsem, device_id=dev, device_id_type=MESH
        )

    def start(copies):
        for copy in copies:
            copy.start()

    def wait(copies):
        for copy in copies:
            copy.wait()

    own = pl.ds(16, 2 * LY)
    wide = pl.ds(8, 48)
    upper, lower = pl.ds(40, 8), pl.ds(16, 8)
    slots = iter(range(64))

    def to(src, dst, where):
        k = next(slots)
        return remote(src, dst, l0_s.at[k], l0_r.at[k], at(*where))

    def ghosts(src, dst, lead, dst_lead, depth):
        x_ends = ((1, LX + 4 - depth, 4 - depth), (-1, 4, LX + 4))
        y_ends = ((1, upper, pl.ds(8, 8)), (-1, lower, pl.ds(48, 8)))
        along_x = [
            to(src.at[lead, pl.ds(a, depth), own], dst.at[dst_lead, pl.ds(b, depth), own], (d, 0)) for d, a, b in x_ends
        ]
        along_y = [
            to(src.at[lead, pl.ds(4, LX), a], dst.at[dst_lead, pl.ds(4, LX), b], (0, d)) for d, a, b in y_ends
        ]
        both = []
        for d, a, _ in x_ends:
            a = LX + 3 if d == 1 else 4
            b = 3 if d == 1 else LX + 4
            for e, p, q in y_ends:
                both.append(to(src.at[lead, pl.ds(a, 1), p], dst.at[dst_lead, pl.ds(b, 1), q], (d, e)))
        return along_x, along_y, both

    def gather(ref, along_gx, ssem, rsem):
        me, count = (gx, gxn) if along_gx else (gy, gyn)

        def peer(i):
            return lax.rem(me + 1 + i, count)

        def send(i, carry):
            dev = (peer(i), gy) if along_gx else (gx, peer(i))
            remote(ref.at[me], ref.at[me], ssem.at[i], rsem.at[me], dev).start()
            return carry

        def finish():
            def take(i, carry):
                dev = (peer(i), gy) if along_gx else (gx, peer(i))
                copy = remote(ref.at[me], ref.at[peer(i)], ssem.at[i], rsem.at[peer(i)], dev)
                copy.wait_send()
                copy.wait_recv()
                return carry

            lax.fori_loop(0, count - 1, take, 0)

        lax.fori_loop(0, count - 1, send, 0)
        return finish

    def iota(shape, dim):
        return lax.broadcasted_iota(jnp.int32, shape, dim)

    def spread(values, x, put):
        even = ((iota((LY, LANES), 0) + x) & 1) == 0
        for h in (0, 1):
            a = values[:, 2 * h * LANES : (2 * h + 1) * LANES]
            b = values[:, (2 * h + 1) * LANES : (2 * h + 2) * LANES]
            put(0, h, jnp.where(even, a, b))
            put(1, h, jnp.where(even, b, a))

    def fill(mixed, plane):
        for x in range(LX):

            def put(c, h, values, x=x):
                WB[plane + c, x + 4, pl.ds(16 + h, LY, stride=2), :] = values

            spread(mixed[x * LY : (x + 1) * LY], x, put)

    for d in range(3):
        flat = coef_ref[d].reshape(LX * LY, 4 * LANES)
        fill(lax.dot_general(flat, pick_ref[...], (((1,), (0,)), ((), ())), preferred_element_type=F32), 2 * d)

    fill(permuted(src_ref[...].reshape(LX * LY, 4 * LANES), pick_ref[...], ((1,), (0,))), 6)
    pl.semaphore_wait(barrier, gxn - 1 + gyn - 1 + 8)

    eight = pl.ds(0, 8)
    wx, wy, wc = ghosts(WB, WB, eight, eight, 1)
    wx.append(to(WB.at[pl.ds(0, 2), LX + 2, own], WB.at[pl.ds(0, 2), 2, own], (1, 0)))
    for e, p, q in ((1, upper, pl.ds(8, 8)), (-1, lower, pl.ds(48, 8))):
        wc.append(to(WB.at[pl.ds(0, 2), LX + 2, p], WB.at[pl.ds(0, 2), 2, q], (1, e)))
    start(wy)
    start(wx)
    start(wc)

    s32 = iota((2 * LY, LANES), 0)
    s48 = iota((48, LANES), 0)
    j8 = iota((8, LANES), 0)
    j12 = iota((12, LANES), 0)
    mine = pl.ds(16, 8)

    def pairs(i, values):
        T[i, pl.ds(0, 32)] = values
        return [T[i, pl.ds(h, 8, stride=4), :] + T[i, pl.ds(h + 2, 8, stride=4), :] for h in (0, 1)]

    def colours(i, two, scale):
        even = ((j8 + i) & 1) == 0
        return jnp.where(even, two[0], two[1]) * scale, jnp.where(even, two[1], two[0]) * scale

    def coarsen(i, carry):
        lo, hi = 4 + 2 * i, 5 + 2 * i
        e, o = colours(i, pairs(i, WB[0, hi, own] + WB[1, hi, own]), 0.0625)
        W1[0, 6 + i, mine] = e
        W1[1, 6 + i, mine] = o
        T[i, pl.ds(0, 32)] = WB[2, lo, own] + WB[3, lo, own] + WB[2, hi, own] + WB[3, hi, own]
        e, o = colours(i, [T[i, pl.ds(2 + h, 8, stride=4), :] for h in (0, 1)], 0.0625)
        W1[2, 6 + i, mine] = e
        W1[3, 6 + i, mine] = o
        even = ((s32 >> 1) & 1) == 0
        low = jnp.where(even, WB[5, lo, own], WB[4, lo, own])
        e, o = colours(i, pairs(i, low + jnp.where(even, WB[4, hi, own], WB[5, hi, own])), 0.0625)
        W1[4, 6 + i, mine] = e
        W1[5, 6 + i, mine] = o
        return carry

    lax.fori_loop(0, 4, coarsen, 0)

    def blocks(src, dst, lead, k):
        near = []
        for i, (dx, dy) in enumerate(around):
            there = dst.at[lead, pl.ds(6 - 4 * dx, 4), pl.ds(16 - 8 * dy, 8)]
            near.append(remote(src.at[lead, pl.ds(6, 4), mine], there, blk_s.at[k, i], blk_r.at[k, i], at(dx, dy)))
        return near

    def second(src, dst, lead, k, sides):
        copies = []
        for dx, a, b in sides:
            for dy in (-1, 0, 1):
                i = 8 + len(copies)
                there = dst.at[lead, pl.ds(b, 1), pl.ds(16 - 8 * dy, 8)]
                copies.append(
                    remote(src.at[lead, pl.ds(a, 1), mine], there, blk_s.at[k, i], blk_r.at[k, i], at(dx, dy))
                )
        return copies

    six, both = pl.ds(0, 6), pl.ds(0, 2)
    w1_copies = blocks(W1, W1, six, 0) + second(W1, W1, pl.ds(0, 2), 0, ((2, 9, 1),))

    sums = [W1[0, 7, mine] + W1[1, 7, mine] + W1[0, 9, mine] + W1[1, 9, mine]]
    part_y, part_z = 0.0, 0.0
    for i in range(4):
        part_y = part_y + jnp.where((j8 & 1) == 1, W1[2, 6 + i, mine] + W1[3, 6 + i, mine], 0.0)
        part_z = part_z + jnp.where(((j8 + i) & 1) == 0, W1[5, 6 + i, mine], W1[4, 6 + i, mine])
    sums += [part_y, part_z]
    scale = 1.0 / (16.0 * 2 * gxn * 4 * gyn * LANES)
    lane = iota((1, LANES), 1)
    row = jnp.zeros((1, LANES), F32)
    for d in range(3):
        value = jnp.sum(jnp.sum(sums[d], axis=0, keepdims=True), axis=1, keepdims=True)
        row = row + jnp.where(lane == d, value * scale, 0.0)
    S1[gy] = row

    def other(read, count, pc0):
        h_zero = (iota((count, LANES), 0) & 1) == 0
        up, down = read(1), read(-1)
        return jnp.where(
            h_zero,
            jnp.where(pc0, pltpu.roll(up, 1, 1), up),
            jnp.where(pc0, down, pltpu.roll(down, LANES - 1, 1)),
        )

    def coefficients(x, carry):
        for c in (0, 1):
            o = 1 - c
            pc0 = (((s48 >> 1) + x + c) & 1) == 0
            xp, xm = WB[c, x, wide], WB[o, x - 1, wide]
            yp, ym = WB[2 + c, x, wide], WB[2 + o, x, pl.ds(6, 48)]
            zc, zo = WB[4 + c, x, wide], WB[4 + o, x, wide]
            zs = jnp.where(pc0, zc, zo)
            far = other(lambda ds: WB[4 + o, x, pl.ds(8 + ds, 48)], 48, pc0)
            zt = jnp.where(pc0, far, zc)
            diagonal = MASS + xp + xm + yp + ym + zs + zt
            inverse = 1.0 / diagonal
            for k, value in enumerate((xp, xm, yp, ym, zs, zt)):
                C[c, k, x] = value * inverse
            DG[c, x] = diagonal
            g = WB[6 + c, x, wide] * inverse
            G[c, x] = g
            if c == 0:
                V[0, x, wide] = g
        return carry

    def weighted(A, c, x, base, count):
        o = 1 - c
        at_base, here = pl.ds(base - 8, count), pl.ds(base, count)
        pc0 = (((iota((count, LANES), 0) >> 1) + x + c) & 1) == 0
        total = G[c, x, at_base] + C[c, 0, x, at_base] * A[o, x + 1, here] + C[c, 1, x, at_base] * A[o, x - 1, here]
        total = total + C[c, 2, x, at_base] * A[o, x, pl.ds(base + 2, count)]
        total = total + C[c, 3, x, at_base] * A[o, x, pl.ds(base - 2, count)]
        far = other(lambda ds: A[o, x, pl.ds(base + ds, count)], count, pc0)
        return total + C[c, 4, x, at_base] * A[o, x, here] + C[c, 5, x, at_base] * far

    def half_sweep(A, c, into, beyond):
        low, base, count = (3, 8, 48) if beyond else (4, 16, 32)

        def rows(i, carry):
            x = low + i
            into[c, x, pl.ds(base, count)] = weighted(A, c, x, base, count)
            return carry

        lax.fori_loop(0, 16 - 2 * low, rows, 0)

    wait(wy)
    lax.fori_loop(0, 2, lambda i, carry: coefficients(5 + 5 * i, carry), 0)
    ends = [
        to(V.at[0, 10, own], V.at[0, 2, own], (1, 0)),
        to(V.at[0, 5, own], V.at[0, 13, own], (-1, 0)),
    ]
    start(ends)
    lax.fori_loop(6, 10, coefficients, 0)
    lax.fori_loop(11, 12, coefficients, 0)
    wait(wx)
    wait(wc)
    lax.fori_loop(3, 5, coefficients, 0)
    lax.fori_loop(12, 13, coefficients, 0)
    wait(ends)
    half_sweep(V, 1, V, True)
    half_sweep(V, 0, VQ, False)
    ex, ey, ec = ghosts(VQ, VQ, 0, 0, 2)
    start(ex)
    start(ey)
    start(ec)
    start(w1_copies)
    wait_c1 = gather(S1, False, c1_s, c1_r)
    wait(ex)
    wait(ey)
    wait(ec)
    half_sweep(VQ, 1, VQ, True)

    def restrict(i, carry):
        total = None
        for parity in (0, 1):
            x = 4 + 2 * i + parity
            for c in (0, 1):
                r = DG[c, x, pl.ds(8, 32)] * (weighted(VQ, c, x, 16, 32) - VQ[c, x, own])
                total = r if total is None else total + r
        e, o = colours(i, pairs(i, total), 0.125)
        B1[0, 6 + i, mine] = e
        B1[1, 6 + i, mine] = o
        return carry

    lax.fori_loop(0, 4, restrict, 0)
    b1_copies = blocks(B1, B1, both, 1)
    start(b1_copies)

    wait_c1()
    S2[gx] = jnp.sum(S1[...], axis=0)
    wait_c2 = gather(S2, True, c2_s, c2_r)

    wait(w1_copies)
    near1 = pl.ds(8, 24)
    s24 = iota((24, LANES), 0)

    def coefficients1(x, carry):
        for c in (0, 1):
            o = 1 - c
            pc0 = ((s24 + x + c) & 1) == 0
            zc, zo = W1[4 + c, x, near1], W1[4 + o, x, near1]
            zs, zt = jnp.where(pc0, zc, zo), jnp.where(pc0, pltpu.roll(zo, 1, 1), zc)
            values = (W1[c, x, near1], W1[o, x - 1, near1], W1[2 + c, x, near1], W1[2 + o, x, pl.ds(7, 24)], zs, zt)
            diagonal = MASS
            for value in values:
                diagonal = diagonal + value
            inverse = 1.0 / diagonal
            D1[c, x] = diagonal
            I1[c, x] = inverse
            for k, value in enumerate(values):
                C1[c, k, x] = value * inverse
        return carry

    lax.fori_loop(2, 14, coefficients1, 0)

    def weighted1(A, c, x):
        o = 1 - c
        pc0 = ((s24 + x + c) & 1) == 0
        here = A[o, x, near1]
        total = B1[c, x, near1] * I1[c, x] + C1[c, 0, x] * A[o, x + 1, near1] + C1[c, 1, x] * A[o, x - 1, near1]
        total = total + C1[c, 2, x] * A[o, x, pl.ds(9, 24)] + C1[c, 3, x] * A[o, x, pl.ds(7, 24)]
        far = jnp.where(pc0, pltpu.roll(here, 1, 1), pltpu.roll(here, LANES - 1, 1))
        return total + C1[c, 4, x] * here + C1[c, 5, x] * far

    def half_sweep1(A, c, low):
        def rows(i, carry):
            x = low + i
            A[c, x, near1] = weighted1(A, c, x)
            return carry

        lax.fori_loop(0, 16 - 2 * low, rows, 0)

    wait(b1_copies)

    def first1(x, carry):
        V1[0, x, near1] = B1[0, x, near1] * I1[0, x]
        return carry

    lax.fori_loop(2, 14, first1, 0)
    half_sweep1(V1, 1, 3)
    half_sweep1(V1, 0, 4)
    half_sweep1(V1, 1, 5)

    for i in range(2):
        total = None
        for k in range(2):
            x = 6 + 2 * i + k
            for c in (0, 1):
                r = ((weighted1(V1, c, x) - V1[c, x, near1]) * D1[c, x])[8:16]
                total = r if total is None else total + r
        T1[pl.ds(8, 8), :] = total
        Z[pl.ds(4 * i, 4), :] = (T1[pl.ds(8, 4, stride=2), :] + T1[pl.ds(9, 4, stride=2), :]) * 0.125

    G1[gy] = dot(Z[...], depth_ref[...])
    finish = gather(G1, False, g1_s, g1_r)
    one = pl.ds(1, 1)
    v1_copies = blocks(V1, VB, one, 2) + second(V1, VB, one, 2, ((2, 9, 1), (-2, 6, 14)))
    start(v1_copies)
    vx, vy, vc = ghosts(VQ, VP, 1, 1, 2)
    start(vy)

    wait_c2()
    CR[...] = jnp.sum(S2[...], axis=0)
    mean = [jnp.sum(jnp.where(lane == d, CR[...], 0.0), axis=1, keepdims=True) for d in range(3)]
    cells = float(2 * gxn * 4 * gyn * LANES)
    flat_part = MASS + mean[1] * wavey_ref[gy] + mean[2] * wavez_ref[...]

    def eigen(i, carry):
        tile = pl.ds(pl.multiple_of(8 * i, 8), 8)
        DI[tile, :] = 1.0 / ((flat_part + mean[0] * wavex_ref[tile, :]) * cells)
        return carry

    lax.fori_loop(0, gxn, eigen, 0)
    VB[1, pl.ds(6, 4), mine] = V1[1, pl.ds(6, 4), mine]
    VP[1, pl.ds(4, LX), own] = VQ[1, pl.ds(4, LX), own]
    finish()
    G2[gx] = dot(first_ref[gy], G1[...].reshape(8 * gyn, LANES))
    finish = gather(G2, True, g2_s, g2_r)
    start(vx)
    start(vc)
    table_copy.wait()
    column_x = (iota((16, 32 * gyn), 1) >> 2) & 7
    for x in range(8):
        M3[pl.ds(16 * x, 16), :] = jnp.where(column_x == x, LT[...], 0.0)
    finish()
    spectrum = dot(alongx_ref[...], G2[...].reshape(8 * gxn, LANES)) * DI[...]
    back_x = dot(padx_ref[pl.ds(pl.multiple_of(8 * gx, 8), 32), :], spectrum)
    G3[gy] = dot(back_x, depth_ref[...])
    finish = gather(G3, False, g3_s, g3_r)
    wait(v1_copies)
    wait(vy)
    wait(vx)
    wait(vc)
    finish()
    coarse = dot(M3[...], G3[...].reshape(32 * gyn, LANES))

    for a in range(8):
        part = coarse[16 * a : 16 * a + 16]
        T1[pl.ds(2, 16, stride=2), :] = part
        T1[pl.ds(3, 16, stride=2), :] = part
        for x in (2 * a, 2 * a + 1):
            VB[1, x, near1] = VB[1, x, near1] + T1[pl.ds(0, 24), :]
    half_sweep1(VB, 0, 2)
    half_sweep1(VB, 1, 3)
    half_sweep1(VB, 0, 4)
    half_sweep1(VB, 1, 5)

    def prolong(i, carry):
        even = ((j12 + i) & 1) == 0
        e, o = VB[0, 4 + i, pl.ds(14, 12)], VB[1, 4 + i, pl.ds(14, 12)]
        for h, part in enumerate((jnp.where(even, e, o), jnp.where(even, o, e))):
            T[i, pl.ds(h, 12, stride=4), :] = part
            T[i, pl.ds(h + 2, 12, stride=4), :] = part
        for x in (2 * i, 2 * i + 1):
            VP[1, x, wide] = VP[1, x, wide] + T[i]
        return carry

    lax.fori_loop(1, 7, prolong, 0)
    half_sweep(VP, 0, VP, True)
    half_sweep(VP, 1, V, False)
    ex, ey, ec = ghosts(V, V, 1, 1, 2)
    start(ex)
    start(ey)
    start(ec)
    wait(ex)
    wait(ey)
    wait(ec)
    half_sweep(V, 0, V, True)
    half_sweep(V, 1, V, False)

    for x in range(LX):
        even = ((iota((LY, LANES), 0) + x) & 1) == 0
        for h in (0, 1):
            e, o = V[0, x + 4, pl.ds(16 + h, LY, stride=2), :], V[1, x + 4, pl.ds(16 + h, LY, stride=2), :]
            rows = pl.ds(x * LY, LY)
            Q[rows, pl.ds(2 * h * LANES, LANES)] = jnp.where(even, e, o)
            Q[rows, pl.ds((2 * h + 1) * LANES, LANES)] = jnp.where(even, o, e)
    out_ref[...] = permuted(Q[...], pick_ref[...], ((1,), (1,))).reshape(LX, LY, 4 * LANES)


def solution(mesh):
    gxn, gyn = mesh.shape["gx"], mesh.shape["gy"]
    consts = tables(gxn, gyn)

    def step(source, face_coef):
        vmem = pl.BlockSpec(memory_space=pltpu.VMEM)
        dma = pltpu.SemaphoreType.DMA
        V = pltpu.VMEM
        return pl.pallas_call(
            functools.partial(kernel, gxn, gyn),
            out_shape=jax.ShapeDtypeStruct((LX, LY, 4 * LANES), F32),
            in_specs=[vmem] * 6 + [pl.BlockSpec(memory_space=pl.ANY)] + [vmem] * 4,
            out_specs=vmem,
            scratch_shapes=[
                V((8, 16, 64, LANES), F32),
                V((2, 16, 64, LANES), F32),
                V((2, 16, 64, LANES), F32),
                V((2, 16, 64, LANES), F32),
                V((2, 6, 16, 48, LANES), F32),
                V((2, 16, 48, LANES), F32),
                V((2, 16, 48, LANES), F32),
                V((8, 48, LANES), F32),
                V((6, 16, 40, LANES), F32),
                V((2, 16, 24, LANES), F32),
                V((2, 16, 24, LANES), F32),
                V((2, 6, 16, 24, LANES), F32),
                V((2, 16, 40, LANES), F32),
                V((2, 16, 40, LANES), F32),
                V((2, 16, 40, LANES), F32),
                V((40, LANES), F32),
                V((8, LANES), F32),
                V((gyn, 8, LANES), F32),
                V((gxn, 8, LANES), F32),
                V((gyn, 32, LANES), F32),
                V((8 * gxn, LANES), F32),
                V((gyn, 1, LANES), F32),
                V((gxn, 1, LANES), F32),
                V((1, LANES), F32),
                V((LX * LY, 4 * LANES), F32),
                V((16, 32 * gyn), F32),
                V((128, 32 * gyn), F32),
                dma((48,)),
                dma((48,)),
                dma((3, 14)),
                dma((3, 14)),
                dma((gyn,)),
                dma((gyn,)),
                dma((gxn,)),
                dma((gxn,)),
                dma((gyn,)),
                dma((gyn,)),
                dma((gyn,)),
                dma((gyn,)),
                dma((gxn,)),
                dma((gxn,)),
                dma,
            ],
            compiler_params=pltpu.CompilerParams(
                collective_id=0, has_side_effects=True, vmem_limit_bytes=60 * 1024 * 1024
            ),
            name="cycle",
        )(source, face_coef, *[jnp.asarray(t) for t in consts])

    return jax.shard_map(
        step,
        mesh=mesh,
        in_specs=(P("gx", "gy", None), P(None, "gx", "gy", None)),
        out_specs=P("gx", "gy", None),
        check_vma=False,
    )
```

```python
import functools

import jax
import jax.numpy as jnp
import numpy as np
from jax import lax
from jax.experimental import pallas as pl
from jax.experimental.pallas import tpu as pltpu
from jax.sharding import PartitionSpec as P

MASS = 0.002
LX, LY = 8, 16
LANES = 128
MESH = pl.DeviceIdType.MESH
F32 = jnp.float32


def cas(rows, cols, length):
    angle = 2.0 * np.pi * ((rows * cols) % length) / length
    return np.cos(angle) + np.sin(angle)


@functools.lru_cache(maxsize=4)
def tables(gxn, gyn):
    nx, ny = 2 * gxn, 4 * gyn
    lanes = np.arange(LANES)
    depth = cas(lanes[:, None], lanes[None, :], LANES)
    rows = np.arange(nx)
    along_x = np.kron(cas(rows[:, None], rows[None, :], nx), np.eye(4))
    padded = along_x[(np.arange(4 * nx + 24) - 12) % (4 * nx)]
    cols = np.arange(ny)
    first = np.zeros((gyn, 2, 4, gyn, 2, 4))
    last = np.zeros((gyn, 16, gyn, 8, 4))
    for me in range(gyn):
        table = cas((4 * me + np.arange(4))[:, None], cols[None, :], ny).reshape(4, gyn, 4)
        for i in range(2):
            first[me, i, :, :, i, :] = table
        table = cas(((4 * me - 3 + np.arange(16)) % ny)[:, None], cols[None, :], ny).reshape(16, gyn, 4)
        last[me] = table[:, :, None, :]
    first = first.reshape(gyn, 8, gyn * 8)
    last = last.reshape(gyn, 16, gyn * 32)
    wave_x = np.repeat(2.0 - 2.0 * np.cos(2.0 * np.pi * rows / nx), 4)[:, None] * np.ones((1, LANES))
    ky = 4 * np.arange(gyn)[:, None] + np.tile(np.arange(4), 2)[None, :]
    wave_y = (2.0 - 2.0 * np.cos(2.0 * np.pi * ky / ny))[:, :, None] * np.ones((1, 1, LANES))
    wave_z = (2.0 - 2.0 * np.cos(2.0 * np.pi * lanes / LANES))[None, :] * np.ones((8, 1))
    pick = np.zeros((4 * LANES, 4 * LANES))
    column = np.arange(4 * LANES)
    pick[4 * (column % LANES) + column // LANES, column] = 1.0
    stacked = np.concatenate([depth, wave_x, wave_z])
    both_x = np.concatenate([along_x, padded])
    out = [np.asarray(t, np.float32) for t in (stacked, both_x, first, last, wave_y)]
    return out + [pick.astype(jnp.bfloat16)]


def permuted(values, pick, dims):
    total = None
    rest = values
    for _ in range(3):
        part = rest.astype(jnp.bfloat16)
        rest = rest - part.astype(F32)
        term = lax.dot_general(part, pick, (dims, ((), ())), preferred_element_type=F32)
        total = term if total is None else total + term
    return total


def dot(a, b):
    return lax.dot_general(
        a, b, (((1,), (0,)), ((), ())), precision=lax.Precision.HIGHEST, preferred_element_type=F32
    )


def kernel(
    gxn,
    gyn,
    src_ref,
    coef_ref,
    stacked_hbm,
    alongx_hbm,
    first_hbm,
    last_hbm,
    wavey_hbm,
    pick_ref,
    out_ref,
    WB,
    V,
    VQ,
    VP,
    C,
    G,
    DG,
    T,
    W1,
    D1,
    I1,
    C1,
    B1,
    V1,
    VB,
    T1,
    Z,
    G1,
    G2,
    G3,
    DI,
    S1,
    S2,
    CR,
    Q,
    LT,
    M3,
    GE,
    STK,
    AX,
    FI,
    WY,
    SPARE,
    group_s,
    group_r,
    local,
):
    gx = lax.axis_index("gx")
    gy = lax.axis_index("gy")

    def at(dx, dy):
        return (lax.rem(gx + dx + gxn, gxn), lax.rem(gy + dy + gyn, gyn))

    corners = [(dx, dy) for dx in (1, -1) for dy in (1, -1)]
    around = [(1, 0), (-1, 0), (0, 1), (0, -1)] + corners

    barrier = pltpu.get_barrier_semaphore()
    for dx, dy in corners:
        for far in (1, 2):
            pl.semaphore_signal(barrier, inc=1, device_id=at(far * dx, dy), device_id_type=MESH)

    def greet_x(i, carry):
        pl.semaphore_signal(barrier, inc=1, device_id=(lax.rem(gx + 1 + i, gxn), gy), device_id_type=MESH)
        return carry

    def greet_y(i, carry):
        pl.semaphore_signal(barrier, inc=1, device_id=(gx, lax.rem(gy + 1 + i, gyn)), device_id_type=MESH)
        return carry

    lax.fori_loop(0, gxn - 1, greet_x, 0)
    lax.fori_loop(0, gyn - 1, greet_y, 0)

    table_copies = [
        pltpu.make_async_copy(a, b, local.at[i])
        for i, (a, b) in enumerate(
            ((last_hbm.at[gy], LT), (stacked_hbm, STK), (alongx_hbm, AX), (first_hbm.at[gy], FI), (wavey_hbm.at[gy], WY))
        )
    ]
    for copy in table_copies:
        copy.start()

    def remote(src, dst, ssem, rsem, dev):
        return pltpu.make_async_remote_copy(
            src_ref=src, dst_ref=dst, send_sem=ssem, recv_sem=rsem, device_id=dev, device_id_type=MESH
        )

    groups = iter(range(32))

    class Group:
        def __init__(self):
            k = next(groups)
            self.send, self.recv, self.rows = group_s.at[k], group_r.at[k], 0

        def start(self, copies):
            for src, dst, where in copies:
                self.rows += int(np.prod(src.shape)) // LANES
                remote(src, dst, self.send, self.recv, at(*where)).start()

        def wait(self):
            whole = SPARE.at[pl.ds(0, self.rows)]
            copy = remote(whole, whole, self.send, self.recv, at(1, 0))
            copy.wait_send()
            copy.wait_recv()

    own = pl.ds(16, 2 * LY)
    wide = pl.ds(8, 48)
    upper, lower = pl.ds(40, 8), pl.ds(16, 8)
    def ghosts(src, dst, lead, dst_lead, depth):
        x_ends = ((1, LX + 4 - depth, 4 - depth), (-1, 4, LX + 4))
        y_ends = ((1, upper, pl.ds(8, 8)), (-1, lower, pl.ds(48, 8)))
        along_x = [
            (src.at[lead, pl.ds(a, depth), own], dst.at[dst_lead, pl.ds(b, depth), own], (d, 0)) for d, a, b in x_ends
        ]
        along_y = [
            (src.at[lead, pl.ds(4, LX), a], dst.at[dst_lead, pl.ds(4, LX), b], (0, d)) for d, a, b in y_ends
        ]
        both = []
        for d, a, _ in x_ends:
            a = LX + 3 if d == 1 else 4
            b = 3 if d == 1 else LX + 4
            for e, p, q in y_ends:
                both.append((src.at[lead, pl.ds(a, 1), p], dst.at[dst_lead, pl.ds(b, 1), q], (d, e)))
        return along_x, along_y, both

    def gather(ref, along_gx):
        me, count = (gx, gxn) if along_gx else (gy, gyn)
        k = next(groups)

        def send(i, carry):
            peer = lax.rem(me + 1 + i, count)
            dev = (peer, gy) if along_gx else (gx, peer)
            remote(ref.at[me], ref.at[me], group_s.at[k], group_r.at[k], dev).start()
            return carry

        def finish():
            whole = ref.at[pl.ds(0, count - 1)]
            copy = remote(whole, whole, group_s.at[k], group_r.at[k], at(1, 0))
            copy.wait_send()
            copy.wait_recv()

        lax.fori_loop(0, count - 1, send, 0)
        return finish

    def iota(shape, dim):
        return lax.broadcasted_iota(jnp.int32, shape, dim)

    def spread(values, x, put):
        even = ((iota((LY, LANES), 0) + x) & 1) == 0
        for h in (0, 1):
            a = values[:, 2 * h * LANES : (2 * h + 1) * LANES]
            b = values[:, (2 * h + 1) * LANES : (2 * h + 2) * LANES]
            put(0, h, jnp.where(even, a, b))
            put(1, h, jnp.where(even, b, a))

    def fill(mixed, plane):
        for x in range(LX):

            def put(c, h, values, x=x):
                WB[plane + c, x + 4, pl.ds(16 + h, LY, stride=2), :] = values

            spread(mixed[x * LY : (x + 1) * LY], x, put)

    for d in range(3):
        flat = coef_ref[d].reshape(LX * LY, 4 * LANES)
        fill(lax.dot_general(flat, pick_ref[...], (((1,), (0,)), ((), ())), preferred_element_type=F32), 2 * d)

    fill(permuted(src_ref[...].reshape(LX * LY, 4 * LANES), pick_ref[...], ((1,), (0,))), 6)
    pl.semaphore_wait(barrier, gxn - 1 + gyn - 1 + 8)

    first_y, rest_y, all_x = Group(), Group(), Group()
    low_high = (upper, pl.ds(8, 8)), (lower, pl.ds(48, 8))
    inner = pl.ds(4, LX)
    first_y.start([(WB.at[pl.ds(2, 2), inner, upper], WB.at[pl.ds(2, 2), inner, pl.ds(8, 8)], (0, 1))])
    eight, pair = pl.ds(0, 8), pl.ds(0, 2)
    wx, wy, wc = ghosts(WB, WB, eight, eight, 1)
    all_x.start(wx)
    all_x.start([(WB.at[pair, LX + 2, own], WB.at[pair, 2, own], (1, 0))])
    rest_y.start(
        [(WB.at[p, inner, upper], WB.at[p, inner, pl.ds(8, 8)], (0, 1)) for p in (pair, pl.ds(4, 4))] + wy[1:]
    )
    all_x.start(wc)
    all_x.start([(WB.at[pair, LX + 2, p], WB.at[pair, 2, q], (1, e)) for e, (p, q) in zip((1, -1), low_high)])

    s32 = iota((2 * LY, LANES), 0)
    s48 = iota((48, LANES), 0)
    j8 = iota((8, LANES), 0)
    j12 = iota((12, LANES), 0)
    mine = pl.ds(16, 8)

    def pairs(i, values):
        T[i, pl.ds(0, 32)] = values
        return [T[i, pl.ds(h, 8, stride=4), :] + T[i, pl.ds(h + 2, 8, stride=4), :] for h in (0, 1)]

    def colours(i, two, scale):
        even = ((j8 + i) & 1) == 0
        return jnp.where(even, two[0], two[1]) * scale, jnp.where(even, two[1], two[0]) * scale

    def coarsen(i, carry):
        lo, hi = 4 + 2 * i, 5 + 2 * i
        e, o = colours(i, pairs(i, WB[0, hi, own] + WB[1, hi, own]), 0.0625)
        W1[0, 6 + i, mine] = e
        W1[1, 6 + i, mine] = o
        T[i, pl.ds(0, 32)] = WB[2, lo, own] + WB[3, lo, own] + WB[2, hi, own] + WB[3, hi, own]
        e, o = colours(i, [T[i, pl.ds(2 + h, 8, stride=4), :] for h in (0, 1)], 0.0625)
        W1[2, 6 + i, mine] = e
        W1[3, 6 + i, mine] = o
        even = ((s32 >> 1) & 1) == 0
        low = jnp.where(even, WB[5, lo, own], WB[4, lo, own])
        e, o = colours(i, pairs(i, low + jnp.where(even, WB[4, hi, own], WB[5, hi, own])), 0.0625)
        W1[4, 6 + i, mine] = e
        W1[5, 6 + i, mine] = o
        return carry

    lax.fori_loop(0, 4, coarsen, 0)

    def blocks(src, dst, lead):
        return [
            (src.at[lead, pl.ds(6, 4), mine], dst.at[lead, pl.ds(6 - 4 * dx, 4), pl.ds(16 - 8 * dy, 8)], (dx, dy))
            for dx, dy in around
        ]

    def second(src, dst, lead, sides):
        return [
            (src.at[lead, pl.ds(a, 1), mine], dst.at[lead, pl.ds(b, 1), pl.ds(16 - 8 * dy, 8)], (dx, dy))
            for dx, a, b in sides
            for dy in (-1, 0, 1)
        ]

    six, both = pl.ds(0, 6), pl.ds(0, 2)

    sums = [W1[0, 7, mine] + W1[1, 7, mine] + W1[0, 9, mine] + W1[1, 9, mine]]
    part_y, part_z = 0.0, 0.0
    for i in range(4):
        part_y = part_y + jnp.where((j8 & 1) == 1, W1[2, 6 + i, mine] + W1[3, 6 + i, mine], 0.0)
        part_z = part_z + jnp.where(((j8 + i) & 1) == 0, W1[5, 6 + i, mine], W1[4, 6 + i, mine])
    sums += [part_y, part_z]
    scale = 1.0 / (16.0 * 2 * gxn * 4 * gyn * LANES)
    lane = iota((1, LANES), 1)
    row = jnp.zeros((1, LANES), F32)
    for d in range(3):
        value = jnp.sum(jnp.sum(sums[d], axis=0, keepdims=True), axis=1, keepdims=True)
        row = row + jnp.where(lane == d, value * scale, 0.0)
    S1[gy] = row

    def other(read, count, pc0):
        h_zero = (iota((count, LANES), 0) & 1) == 0
        up, down = read(1), read(-1)
        return jnp.where(
            h_zero,
            jnp.where(pc0, pltpu.roll(up, 1, 1), up),
            jnp.where(pc0, down, pltpu.roll(down, LANES - 1, 1)),
        )

    def coefficients(x, carry):
        for c in (0, 1):
            o = 1 - c
            pc0 = (((s48 >> 1) + x + c) & 1) == 0
            xp, xm = WB[c, x, wide], WB[o, x - 1, wide]
            yp, ym = WB[2 + c, x, wide], WB[2 + o, x, pl.ds(6, 48)]
            zc, zo = WB[4 + c, x, wide], WB[4 + o, x, wide]
            zs = jnp.where(pc0, zc, zo)
            far = other(lambda ds: WB[4 + o, x, pl.ds(8 + ds, 48)], 48, pc0)
            zt = jnp.where(pc0, far, zc)
            diagonal = MASS + xp + xm + yp + ym + zs + zt
            inverse = 1.0 / diagonal
            for k, value in enumerate((xp, xm, yp, ym, zs, zt)):
                C[c, k, x] = value * inverse
            DG[c, x] = diagonal
            g = WB[6 + c, x, wide] * inverse
            G[c, x] = g
            if c == 0:
                V[0, x, wide] = g
        return carry

    def weighted(A, c, x, base, count):
        o = 1 - c
        at_base, here = pl.ds(base - 8, count), pl.ds(base, count)
        pc0 = (((iota((count, LANES), 0) >> 1) + x + c) & 1) == 0
        total = G[c, x, at_base] + C[c, 0, x, at_base] * A[o, x + 1, here] + C[c, 1, x, at_base] * A[o, x - 1, here]
        total = total + C[c, 2, x, at_base] * A[o, x, pl.ds(base + 2, count)]
        total = total + C[c, 3, x, at_base] * A[o, x, pl.ds(base - 2, count)]
        far = other(lambda ds: A[o, x, pl.ds(base + ds, count)], count, pc0)
        return total + C[c, 4, x, at_base] * A[o, x, here] + C[c, 5, x, at_base] * far

    def update(A, c, into, low, high, base=16, count=32):
        def rows(x, carry):
            into[c, x, pl.ds(base, count)] = weighted(A, c, x, base, count)
            return carry

        lax.fori_loop(low, high, rows, 0)

    def half_sweep(A, c, into, beyond):
        if beyond:
            update(A, c, into, 3, 13, 8, 48)
        else:
            update(A, c, into, 4, 12)

    def ends(i, carry):
        x = 5 + 5 * i
        pc0 = (((s32 >> 1) + x) & 1) == 0
        diagonal = MASS + WB[0, x, own] + WB[1, x - 1, own] + WB[2, x, own] + WB[3, x, pl.ds(14, 32)]
        far = WB[5, x, own]
        far = other(lambda ds: pltpu.roll(far, (2 * LY - ds) % (2 * LY), 0), 32, pc0)
        diagonal = diagonal + jnp.where(pc0, WB[4, x, own], WB[5, x, own]) + jnp.where(pc0, far, WB[4, x, own])
        GE[i] = WB[6, x, own] / diagonal
        return carry

    first_y.wait()
    lax.fori_loop(0, 2, ends, 0)
    outer = Group()
    outer.start([(GE.at[1], V.at[0, 2, own], (1, 0)), (GE.at[0], V.at[0, 13, own], (-1, 0))])
    w1_group = Group()
    w1_group.start(blocks(W1, W1, six) + second(W1, W1, pair, ((2, 9, 1),)))
    wait_c1 = gather(S1, False)
    rest_y.wait()
    lax.fori_loop(5, 12, coefficients, 0)
    all_x.wait()
    lax.fori_loop(3, 5, coefficients, 0)
    lax.fori_loop(12, 13, coefficients, 0)
    outer.wait()
    half_sweep(V, 1, V, True)

    def exchanged(A, c, into):
        layers = Group()
        ex, ey, ec = ghosts(into, into, c, c, 2)
        update(A, c, into, 4, 6)
        update(A, c, into, 10, 12)
        layers.start(ex + ec)
        update(A, c, into, 6, 10)
        layers.start(ey)
        layers.wait()

    exchanged(V, 0, VQ)
    half_sweep(VQ, 1, VQ, True)

    def restrict(i, carry):
        total = None
        for parity in (0, 1):
            x = 4 + 2 * i + parity
            for c in (0, 1):
                r = DG[c, x, pl.ds(8, 32)] * (weighted(VQ, c, x, 16, 32) - VQ[c, x, own])
                total = r if total is None else total + r
        e, o = colours(i, pairs(i, total), 0.125)
        B1[0, 6 + i, mine] = e
        B1[1, 6 + i, mine] = o
        return carry

    lax.fori_loop(0, 4, restrict, 0)
    b1_group = Group()
    b1_group.start(blocks(B1, B1, both))

    wait_c1()
    S2[gx] = jnp.sum(S1[...], axis=0)
    wait_c2 = gather(S2, True)

    w1_group.wait()
    near1 = pl.ds(8, 24)
    s24 = iota((24, LANES), 0)

    def coefficients1(x, carry):
        for c in (0, 1):
            o = 1 - c
            pc0 = ((s24 + x + c) & 1) == 0
            zc, zo = W1[4 + c, x, near1], W1[4 + o, x, near1]
            zs, zt = jnp.where(pc0, zc, zo), jnp.where(pc0, pltpu.roll(zo, 1, 1), zc)
            values = (W1[c, x, near1], W1[o, x - 1, near1], W1[2 + c, x, near1], W1[2 + o, x, pl.ds(7, 24)], zs, zt)
            diagonal = MASS
            for value in values:
                diagonal = diagonal + value
            inverse = 1.0 / diagonal
            D1[c, x] = diagonal
            I1[c, x] = inverse
            for k, value in enumerate(values):
                C1[c, k, x] = value * inverse
        return carry

    lax.fori_loop(2, 14, coefficients1, 0)

    def weighted1(A, c, x):
        o = 1 - c
        pc0 = ((s24 + x + c) & 1) == 0
        here = A[o, x, near1]
        total = B1[c, x, near1] * I1[c, x] + C1[c, 0, x] * A[o, x + 1, near1] + C1[c, 1, x] * A[o, x - 1, near1]
        total = total + C1[c, 2, x] * A[o, x, pl.ds(9, 24)] + C1[c, 3, x] * A[o, x, pl.ds(7, 24)]
        far = jnp.where(pc0, pltpu.roll(here, 1, 1), pltpu.roll(here, LANES - 1, 1))
        return total + C1[c, 4, x] * here + C1[c, 5, x] * far

    def half_sweep1(A, c, low):
        def rows(i, carry):
            x = low + i
            A[c, x, near1] = weighted1(A, c, x)
            return carry

        lax.fori_loop(0, 16 - 2 * low, rows, 0)

    b1_group.wait()

    def first1(x, carry):
        V1[0, x, near1] = B1[0, x, near1] * I1[0, x]
        return carry

    lax.fori_loop(2, 14, first1, 0)
    half_sweep1(V1, 1, 3)
    half_sweep1(V1, 0, 4)
    half_sweep1(V1, 1, 5)

    for i in range(2):
        total = None
        for k in range(2):
            x = 6 + 2 * i + k
            for c in (0, 1):
                r = ((weighted1(V1, c, x) - V1[c, x, near1]) * D1[c, x])[8:16]
                total = r if total is None else total + r
        T1[pl.ds(8, 8), :] = total
        Z[pl.ds(4 * i, 4), :] = (T1[pl.ds(8, 4, stride=2), :] + T1[pl.ds(9, 4, stride=2), :]) * 0.125

    for copy in table_copies:
        copy.wait()
    depth = pl.ds(0, LANES)
    G1[gy] = dot(Z[...], STK[depth, :])
    finish = gather(G1, False)
    one = pl.ds(1, 1)
    v1_group = Group()
    v1_group.start(blocks(V1, VB, one) + second(V1, VB, one, ((2, 9, 1), (-2, 6, 14))))
    v_group = Group()
    vx, vy, vc = ghosts(VQ, VP, 1, 1, 2)
    v_group.start(vy)

    wait_c2()
    CR[...] = jnp.sum(S2[...], axis=0)
    mean = [jnp.sum(jnp.where(lane == d, CR[...], 0.0), axis=1, keepdims=True) for d in range(3)]
    cells = float(2 * gxn * 4 * gyn * LANES)
    flat_part = MASS + mean[1] * WY[...] + mean[2] * STK[pl.ds(LANES + 8 * gxn, 8), :]

    def eigen(i, carry):
        tile = pl.ds(pl.multiple_of(8 * i, 8), 8)
        DI[tile, :] = 1.0 / ((flat_part + mean[0] * STK[pl.ds(pl.multiple_of(LANES + 8 * i, 8), 8), :]) * cells)
        return carry

    lax.fori_loop(0, gxn, eigen, 0)
    VB[1, pl.ds(6, 4), mine] = V1[1, pl.ds(6, 4), mine]
    VP[1, pl.ds(4, LX), own] = VQ[1, pl.ds(4, LX), own]
    finish()
    G2[gx] = dot(FI[...], G1[...].reshape(8 * gyn, LANES))
    finish = gather(G2, True)
    v_group.start(vx + vc)
    column_x = (iota((16, 32 * gyn), 1) >> 2) & 7
    for x in range(8):
        M3[pl.ds(16 * x, 16), :] = jnp.where(column_x == x, LT[...], 0.0)
    finish()
    spectrum = dot(AX[pl.ds(0, 8 * gxn), :], G2[...].reshape(8 * gxn, LANES)) * DI[...]
    back_x = dot(AX[pl.ds(pl.multiple_of(8 * gxn + 8 * gx, 8), 32), :], spectrum)
    G3[gy] = dot(back_x, STK[depth, :])
    finish = gather(G3, False)
    v1_group.wait()
    v_group.wait()
    finish()
    coarse = dot(M3[...], G3[...].reshape(32 * gyn, LANES))

    for a in range(8):
        part = coarse[16 * a : 16 * a + 16]
        T1[pl.ds(2, 16, stride=2), :] = part
        T1[pl.ds(3, 16, stride=2), :] = part
        for x in (2 * a, 2 * a + 1):
            VB[1, x, near1] = VB[1, x, near1] + T1[pl.ds(0, 24), :]
    half_sweep1(VB, 0, 2)
    half_sweep1(VB, 1, 3)
    half_sweep1(VB, 0, 4)
    half_sweep1(VB, 1, 5)

    def prolong(i, carry):
        even = ((j12 + i) & 1) == 0
        e, o = VB[0, 4 + i, pl.ds(14, 12)], VB[1, 4 + i, pl.ds(14, 12)]
        for h, part in enumerate((jnp.where(even, e, o), jnp.where(even, o, e))):
            T[i, pl.ds(h, 12, stride=4), :] = part
            T[i, pl.ds(h + 2, 12, stride=4), :] = part
        for x in (2 * i, 2 * i + 1):
            VP[1, x, wide] = VP[1, x, wide] + T[i]
        return carry

    lax.fori_loop(1, 7, prolong, 0)
    half_sweep(VP, 0, VP, True)
    exchanged(VP, 1, V)
    half_sweep(V, 0, V, True)
    half_sweep(V, 1, V, False)

    for x in range(LX):
        even = ((iota((LY, LANES), 0) + x) & 1) == 0
        for h in (0, 1):
            e, o = V[0, x + 4, pl.ds(16 + h, LY, stride=2), :], V[1, x + 4, pl.ds(16 + h, LY, stride=2), :]
            rows = pl.ds(x * LY, LY)
            Q[rows, pl.ds(2 * h * LANES, LANES)] = jnp.where(even, e, o)
            Q[rows, pl.ds((2 * h + 1) * LANES, LANES)] = jnp.where(even, o, e)
    out_ref[...] = permuted(Q[...], pick_ref[...], ((1,), (1,))).reshape(LX, LY, 4 * LANES)


def solution(mesh):
    gxn, gyn = mesh.shape["gx"], mesh.shape["gy"]
    consts = tables(gxn, gyn)

    def step(source, face_coef):
        vmem = pl.BlockSpec(memory_space=pltpu.VMEM)
        dma = pltpu.SemaphoreType.DMA
        V = pltpu.VMEM
        return pl.pallas_call(
            functools.partial(kernel, gxn, gyn),
            out_shape=jax.ShapeDtypeStruct((LX, LY, 4 * LANES), F32),
            in_specs=[vmem] * 2 + [pl.BlockSpec(memory_space=pl.ANY)] * 5 + [vmem],
            out_specs=vmem,
            scratch_shapes=[
                V((8, 16, 64, LANES), F32),
                V((2, 16, 64, LANES), F32),
                V((2, 16, 64, LANES), F32),
                V((2, 16, 64, LANES), F32),
                V((2, 6, 16, 48, LANES), F32),
                V((2, 16, 48, LANES), F32),
                V((2, 16, 48, LANES), F32),
                V((8, 48, LANES), F32),
                V((6, 16, 40, LANES), F32),
                V((2, 16, 24, LANES), F32),
                V((2, 16, 24, LANES), F32),
                V((2, 6, 16, 24, LANES), F32),
                V((2, 16, 40, LANES), F32),
                V((2, 16, 40, LANES), F32),
                V((2, 16, 40, LANES), F32),
                V((40, LANES), F32),
                V((8, LANES), F32),
                V((gyn, 8, LANES), F32),
                V((gxn, 8, LANES), F32),
                V((gyn, 32, LANES), F32),
                V((8 * gxn, LANES), F32),
                V((gyn, 1, LANES), F32),
                V((gxn, 1, LANES), F32),
                V((1, LANES), F32),
                V((LX * LY, 4 * LANES), F32),
                V((16, 32 * gyn), F32),
                V((128, 32 * gyn), F32),
                V((2, 32, LANES), F32),
                V((LANES + 8 * gxn + 8, LANES), F32),
                V((16 * gxn + 24, 8 * gxn), F32),
                V((8, 8 * gyn), F32),
                V((8, LANES), F32),
                V((2048, LANES), F32),
                dma((15,)),
                dma((15,)),
                dma((5,)),
            ],
            compiler_params=pltpu.CompilerParams(
                collective_id=0, has_side_effects=True, vmem_limit_bytes=60 * 1024 * 1024
            ),
            name="cycle",
        )(source, face_coef, *[jnp.asarray(t) for t in consts])

    return jax.shard_map(
        step,
        mesh=mesh,
        in_specs=(P("gx", "gy", None), P(None, "gx", "gy", None)),
        out_specs=P("gx", "gy", None),
        check_vma=False,
    )
```

```python
import functools

import jax
import jax.numpy as jnp
import numpy as np
from jax import lax
from jax.experimental import pallas as pl
from jax.experimental.pallas import tpu as pltpu
from jax.sharding import PartitionSpec as P

MASS = 0.002
LX, LY = 8, 16
LANES = 128
MESH = pl.DeviceIdType.MESH
F32 = jnp.float32


def cas(rows, cols, length):
    angle = 2.0 * np.pi * ((rows * cols) % length) / length
    return np.cos(angle) + np.sin(angle)


@functools.lru_cache(maxsize=4)
def tables(gxn, gyn):
    nx, ny = 2 * gxn, 4 * gyn
    lanes = np.arange(LANES)
    depth = cas(lanes[:, None], lanes[None, :], LANES)
    rows = np.arange(nx)
    along_x = np.kron(cas(rows[:, None], rows[None, :], nx), np.eye(4))
    padded = along_x[(np.arange(4 * nx + 24) - 12) % (4 * nx)]
    cols = np.arange(ny)
    first = np.zeros((gyn, 2, 4, gyn, 2, 4))
    last = np.zeros((gyn, 16, gyn, 8, 4))
    for me in range(gyn):
        table = cas((4 * me + np.arange(4))[:, None], cols[None, :], ny).reshape(4, gyn, 4)
        for i in range(2):
            first[me, i, :, :, i, :] = table
        table = cas(((4 * me - 3 + np.arange(16)) % ny)[:, None], cols[None, :], ny).reshape(16, gyn, 4)
        last[me] = table[:, :, None, :]
    first = first.reshape(gyn, 8, gyn * 8)
    last = last.reshape(gyn, 16, gyn * 32)
    wave_x = np.repeat(2.0 - 2.0 * np.cos(2.0 * np.pi * rows / nx), 4)[:, None] * np.ones((1, LANES))
    ky = 4 * np.arange(gyn)[:, None] + np.tile(np.arange(4), 2)[None, :]
    wave_y = (2.0 - 2.0 * np.cos(2.0 * np.pi * ky / ny))[:, :, None] * np.ones((1, 1, LANES))
    wave_z = (2.0 - 2.0 * np.cos(2.0 * np.pi * lanes / LANES))[None, :] * np.ones((8, 1))
    pick = np.zeros((4 * LANES, 4 * LANES))
    column = np.arange(4 * LANES)
    pick[4 * (column % LANES) + column // LANES, column] = 1.0
    stacked = np.concatenate([depth, wave_x, wave_z])
    both_x = np.concatenate([along_x, padded])
    out = [np.asarray(t, np.float32) for t in (stacked, both_x, first, last, wave_y)]
    return out + [pick.astype(jnp.bfloat16)]


def permuted(values, pick, dims):
    total = None
    rest = values
    for _ in range(3):
        part = rest.astype(jnp.bfloat16)
        rest = rest - part.astype(F32)
        term = lax.dot_general(part, pick, (dims, ((), ())), preferred_element_type=F32)
        total = term if total is None else total + term
    return total


def dot(a, b):
    return lax.dot_general(
        a, b, (((1,), (0,)), ((), ())), precision=lax.Precision.HIGHEST, preferred_element_type=F32
    )


def kernel(
    gxn,
    gyn,
    src_ref,
    coef_ref,
    stacked_hbm,
    alongx_hbm,
    first_hbm,
    last_hbm,
    wavey_hbm,
    pick_ref,
    out_ref,
    WB,
    V,
    VQ,
    VP,
    C,
    G,
    DG,
    T,
    W1,
    D1,
    I1,
    C1,
    B1,
    V1,
    VB,
    T1,
    Z,
    G1,
    G2,
    G3,
    DI,
    S1,
    S2,
    CR,
    Q,
    LT,
    M3,
    GE,
    STK,
    AX,
    FI,
    WY,
    SPARE,
    group_s,
    group_r,
    local,
):
    gx = lax.axis_index("gx")
    gy = lax.axis_index("gy")

    def at(dx, dy):
        return (lax.rem(gx + dx + gxn, gxn), lax.rem(gy + dy + gyn, gyn))

    corners = [(dx, dy) for dx in (1, -1) for dy in (1, -1)]
    around = [(1, 0), (-1, 0), (0, 1), (0, -1)] + corners

    barrier = pltpu.get_barrier_semaphore()
    for dx, dy in corners:
        for far in (1, 2):
            pl.semaphore_signal(barrier, inc=1, device_id=at(far * dx, dy), device_id_type=MESH)

    def greet_x(i, carry):
        pl.semaphore_signal(barrier, inc=1, device_id=(lax.rem(gx + 1 + i, gxn), gy), device_id_type=MESH)
        return carry

    def greet_y(i, carry):
        pl.semaphore_signal(barrier, inc=1, device_id=(gx, lax.rem(gy + 1 + i, gyn)), device_id_type=MESH)
        return carry

    lax.fori_loop(0, gxn - 1, greet_x, 0)
    lax.fori_loop(0, gyn - 1, greet_y, 0)

    table_copies = [
        pltpu.make_async_copy(a, b, local.at[i])
        for i, (a, b) in enumerate(
            ((last_hbm.at[gy], LT), (stacked_hbm, STK), (alongx_hbm, AX), (first_hbm.at[gy], FI), (wavey_hbm.at[gy], WY))
        )
    ]
    for copy in table_copies:
        copy.start()

    def remote(src, dst, ssem, rsem, dev):
        return pltpu.make_async_remote_copy(
            src_ref=src, dst_ref=dst, send_sem=ssem, recv_sem=rsem, device_id=dev, device_id_type=MESH
        )

    groups = iter(range(32))

    class Group:
        def __init__(self):
            k = next(groups)
            self.send, self.recv, self.rows = group_s.at[k], group_r.at[k], 0

        def start(self, copies):
            for src, dst, where in copies:
                self.rows += int(np.prod(src.shape)) // LANES
                remote(src, dst, self.send, self.recv, at(*where)).start()

        def wait(self):
            whole = SPARE.at[pl.ds(0, self.rows)]
            copy = remote(whole, whole, self.send, self.recv, at(1, 0))
            copy.wait_send()
            copy.wait_recv()

    own = pl.ds(16, 2 * LY)
    wide = pl.ds(8, 48)
    upper, lower = pl.ds(40, 8), pl.ds(16, 8)
    def ghosts(src, dst, lead, dst_lead, depth):
        x_ends = ((1, LX + 4 - depth, 4 - depth), (-1, 4, LX + 4))
        y_ends = ((1, upper, pl.ds(8, 8)), (-1, lower, pl.ds(48, 8)))
        along_x = [
            (src.at[lead, pl.ds(a, depth), own], dst.at[dst_lead, pl.ds(b, depth), own], (d, 0)) for d, a, b in x_ends
        ]
        along_y = [
            (src.at[lead, pl.ds(4, LX), a], dst.at[dst_lead, pl.ds(4, LX), b], (0, d)) for d, a, b in y_ends
        ]
        both = []
        for d, a, _ in x_ends:
            a = LX + 3 if d == 1 else 4
            b = 3 if d == 1 else LX + 4
            for e, p, q in ((1, pl.ds(44, 4), pl.ds(12, 4)), (-1, pl.ds(16, 4), pl.ds(48, 4))):
                both.append((src.at[lead, pl.ds(a, 1), p], dst.at[dst_lead, pl.ds(b, 1), q], (d, e)))
        return along_x, along_y, both

    def gather(ref, along_gx):
        me, count = (gx, gxn) if along_gx else (gy, gyn)
        k = next(groups)

        def send(i, carry):
            peer = lax.rem(me + 1 + i, count)
            dev = (peer, gy) if along_gx else (gx, peer)
            remote(ref.at[me], ref.at[me], group_s.at[k], group_r.at[k], dev).start()
            return carry

        def finish():
            whole = ref.at[pl.ds(0, count - 1)]
            copy = remote(whole, whole, group_s.at[k], group_r.at[k], at(1, 0))
            copy.wait_send()
            copy.wait_recv()

        lax.fori_loop(0, count - 1, send, 0)
        return finish

    def iota(shape, dim):
        return lax.broadcasted_iota(jnp.int32, shape, dim)

    def spread(values, x, put):
        even = ((iota((LY, LANES), 0) + x) & 1) == 0
        for h in (0, 1):
            a = values[:, 2 * h * LANES : (2 * h + 1) * LANES]
            b = values[:, (2 * h + 1) * LANES : (2 * h + 2) * LANES]
            put(0, h, jnp.where(even, a, b))
            put(1, h, jnp.where(even, b, a))

    def fill(mixed, plane):
        for x in range(LX):

            def put(c, h, values, x=x):
                WB[plane + c, x + 4, pl.ds(16 + h, LY, stride=2), :] = values

            spread(mixed[x * LY : (x + 1) * LY], x, put)

    for d in range(3):
        flat = coef_ref[d].reshape(LX * LY, 4 * LANES)
        fill(lax.dot_general(flat, pick_ref[...], (((1,), (0,)), ((), ())), preferred_element_type=F32), 2 * d)

    fill(permuted(src_ref[...].reshape(LX * LY, 4 * LANES), pick_ref[...], ((1,), (0,))), 6)
    pl.semaphore_wait(barrier, gxn - 1 + gyn - 1 + 8)

    first_y, rest_y, all_x = Group(), Group(), Group()
    low_high = (pl.ds(44, 4), pl.ds(12, 4)), (pl.ds(16, 4), pl.ds(48, 4))
    inner = pl.ds(4, LX)
    first_y.start([(WB.at[pl.ds(2, 2), inner, upper], WB.at[pl.ds(2, 2), inner, pl.ds(8, 8)], (0, 1))])
    eight, pair = pl.ds(0, 8), pl.ds(0, 2)
    wx, wy, wc = ghosts(WB, WB, eight, eight, 1)
    all_x.start(wx)
    all_x.start([(WB.at[pair, LX + 2, own], WB.at[pair, 2, own], (1, 0))])
    rest_y.start(
        [(WB.at[p, inner, upper], WB.at[p, inner, pl.ds(8, 8)], (0, 1)) for p in (pair, pl.ds(4, 4))] + wy[1:]
    )
    all_x.start(wc)
    all_x.start([(WB.at[pair, LX + 2, p], WB.at[pair, 2, q], (1, e)) for e, (p, q) in zip((1, -1), low_high)])

    s32 = iota((2 * LY, LANES), 0)
    s48 = iota((48, LANES), 0)
    j8 = iota((8, LANES), 0)
    j12 = iota((12, LANES), 0)
    mine = pl.ds(16, 8)

    def pairs(i, values):
        T[i, pl.ds(0, 32)] = values
        return [T[i, pl.ds(h, 8, stride=4), :] + T[i, pl.ds(h + 2, 8, stride=4), :] for h in (0, 1)]

    def colours(i, two, scale):
        even = ((j8 + i) & 1) == 0
        return jnp.where(even, two[0], two[1]) * scale, jnp.where(even, two[1], two[0]) * scale

    def coarsen(i, carry):
        lo, hi = 4 + 2 * i, 5 + 2 * i
        e, o = colours(i, pairs(i, WB[0, hi, own] + WB[1, hi, own]), 0.0625)
        W1[0, 6 + i, mine] = e
        W1[1, 6 + i, mine] = o
        T[i, pl.ds(0, 32)] = WB[2, lo, own] + WB[3, lo, own] + WB[2, hi, own] + WB[3, hi, own]
        e, o = colours(i, [T[i, pl.ds(2 + h, 8, stride=4), :] for h in (0, 1)], 0.0625)
        W1[2, 6 + i, mine] = e
        W1[3, 6 + i, mine] = o
        even = ((s32 >> 1) & 1) == 0
        low = jnp.where(even, WB[5, lo, own], WB[4, lo, own])
        e, o = colours(i, pairs(i, low + jnp.where(even, WB[4, hi, own], WB[5, hi, own])), 0.0625)
        W1[4, 6 + i, mine] = e
        W1[5, 6 + i, mine] = o
        return carry

    lax.fori_loop(0, 4, coarsen, 0)

    def blocks(src, dst, lead):
        copies = []
        for dx, dy in around:
            a, count = 16, 8
            if dx and dy:
                a, count = (19, 5) if dy == 1 else (16, 5)
            there = dst.at[lead, pl.ds(6 - 4 * dx, 4), pl.ds(a - 8 * dy, count)]
            copies.append((src.at[lead, pl.ds(6, 4), pl.ds(a, count)], there, (dx, dy)))
        return copies

    def second(src, dst, lead, sides):
        return [
            (src.at[lead, pl.ds(a, 1), mine], dst.at[lead, pl.ds(b, 1), pl.ds(16 - 8 * dy, 8)], (dx, dy))
            for dx, a, b in sides
            for dy in (-1, 0, 1)
        ]

    six, both = pl.ds(0, 6), pl.ds(0, 2)

    sums = [W1[0, 7, mine] + W1[1, 7, mine] + W1[0, 9, mine] + W1[1, 9, mine]]
    part_y, part_z = 0.0, 0.0
    for i in range(4):
        part_y = part_y + jnp.where((j8 & 1) == 1, W1[2, 6 + i, mine] + W1[3, 6 + i, mine], 0.0)
        part_z = part_z + jnp.where(((j8 + i) & 1) == 0, W1[5, 6 + i, mine], W1[4, 6 + i, mine])
    sums += [part_y, part_z]
    scale = 1.0 / (16.0 * 2 * gxn * 4 * gyn * LANES)
    lane = iota((1, LANES), 1)
    row = jnp.zeros((1, LANES), F32)
    for d in range(3):
        value = jnp.sum(jnp.sum(sums[d], axis=0, keepdims=True), axis=1, keepdims=True)
        row = row + jnp.where(lane == d, value * scale, 0.0)
    S1[gy] = row

    def other(read, count, pc0):
        h_zero = (iota((count, LANES), 0) & 1) == 0
        up, down = read(1), read(-1)
        return jnp.where(
            h_zero,
            jnp.where(pc0, pltpu.roll(up, 1, 1), up),
            jnp.where(pc0, down, pltpu.roll(down, LANES - 1, 1)),
        )

    def coefficients(x, carry):
        for c in (0, 1):
            o = 1 - c
            pc0 = (((s48 >> 1) + x + c) & 1) == 0
            xp, xm = WB[c, x, wide], WB[o, x - 1, wide]
            yp, ym = WB[2 + c, x, wide], WB[2 + o, x, pl.ds(6, 48)]
            zc, zo = WB[4 + c, x, wide], WB[4 + o, x, wide]
            zs = jnp.where(pc0, zc, zo)
            far = other(lambda ds: WB[4 + o, x, pl.ds(8 + ds, 48)], 48, pc0)
            zt = jnp.where(pc0, far, zc)
            diagonal = MASS + xp + xm + yp + ym + zs + zt
            inverse = 1.0 / diagonal
            for k, value in enumerate((xp, xm, yp, ym, zs, zt)):
                C[c, k, x] = value * inverse
            DG[c, x] = diagonal
            g = WB[6 + c, x, wide] * inverse
            G[c, x] = g
            if c == 0:
                V[0, x, wide] = g
        return carry

    def weighted(A, c, x, base, count):
        o = 1 - c
        at_base, here = pl.ds(base - 8, count), pl.ds(base, count)
        pc0 = (((iota((count, LANES), 0) >> 1) + x + c) & 1) == 0
        total = G[c, x, at_base] + C[c, 0, x, at_base] * A[o, x + 1, here] + C[c, 1, x, at_base] * A[o, x - 1, here]
        total = total + C[c, 2, x, at_base] * A[o, x, pl.ds(base + 2, count)]
        total = total + C[c, 3, x, at_base] * A[o, x, pl.ds(base - 2, count)]
        far = other(lambda ds: A[o, x, pl.ds(base + ds, count)], count, pc0)
        return total + C[c, 4, x, at_base] * A[o, x, here] + C[c, 5, x, at_base] * far

    def update(A, c, into, low, high, base=16, count=32):
        def rows(x, carry):
            into[c, x, pl.ds(base, count)] = weighted(A, c, x, base, count)
            return carry

        lax.fori_loop(low, high, rows, 0, unroll=(high - low) // 2)

    def half_sweep(A, c, into, beyond):
        if beyond:
            update(A, c, into, 3, 13, 8, 48)
        else:
            update(A, c, into, 4, 12)

    def ends(i, carry):
        x = 5 + 5 * i
        pc0 = (((s32 >> 1) + x) & 1) == 0
        diagonal = MASS + WB[0, x, own] + WB[1, x - 1, own] + WB[2, x, own] + WB[3, x, pl.ds(14, 32)]
        far = WB[5, x, own]
        far = other(lambda ds: pltpu.roll(far, (2 * LY - ds) % (2 * LY), 0), 32, pc0)
        diagonal = diagonal + jnp.where(pc0, WB[4, x, own], WB[5, x, own]) + jnp.where(pc0, far, WB[4, x, own])
        GE[i] = WB[6, x, own] / diagonal
        return carry

    first_y.wait()
    lax.fori_loop(0, 2, ends, 0, unroll=2)
    outer = Group()
    outer.start([(GE.at[1], V.at[0, 2, own], (1, 0)), (GE.at[0], V.at[0, 13, own], (-1, 0))])
    w1_group = Group()
    wait_c1 = gather(S1, False)
    rest_y.wait()
    lax.fori_loop(5, 12, coefficients, 0)
    all_x.wait()
    lax.fori_loop(3, 5, coefficients, 0, unroll=2)
    lax.fori_loop(12, 13, coefficients, 0)
    outer.wait()
    half_sweep(V, 1, V, True)

    def exchanged(A, c, into):
        layers = Group()
        ex, ey, ec = ghosts(into, into, c, c, 2)
        update(A, c, into, 4, 6)
        update(A, c, into, 10, 12)
        layers.start(ex + ec)
        update(A, c, into, 6, 10)
        layers.start(ey)
        if into is VQ:
            w1_group.start(blocks(W1, W1, six) + second(W1, W1, pair, ((2, 9, 1),)))
        layers.wait()

    exchanged(V, 0, VQ)
    half_sweep(VQ, 1, VQ, True)

    def restrict(i, carry):
        total = None
        for parity in (0, 1):
            x = 4 + 2 * i + parity
            for c in (0, 1):
                r = DG[c, x, pl.ds(8, 32)] * (weighted(VQ, c, x, 16, 32) - VQ[c, x, own])
                total = r if total is None else total + r
        e, o = colours(i, pairs(i, total), 0.125)
        B1[0, 6 + i, mine] = e
        B1[1, 6 + i, mine] = o
        return carry

    lax.fori_loop(0, 4, restrict, 0, unroll=2)
    b1_group = Group()
    b1_group.start(blocks(B1, B1, both))
    v_group = Group()
    vx, vy, vc = ghosts(VQ, VP, 1, 1, 2)
    v_group.start(vx + vy + vc)

    wait_c1()
    S2[gx] = jnp.sum(S1[...], axis=0)
    wait_c2 = gather(S2, True)

    w1_group.wait()
    near1 = pl.ds(8, 24)
    s24 = iota((24, LANES), 0)

    def coefficients1(x, carry):
        for c in (0, 1):
            o = 1 - c
            pc0 = ((s24 + x + c) & 1) == 0
            zc, zo = W1[4 + c, x, near1], W1[4 + o, x, near1]
            zs, zt = jnp.where(pc0, zc, zo), jnp.where(pc0, pltpu.roll(zo, 1, 1), zc)
            values = (W1[c, x, near1], W1[o, x - 1, near1], W1[2 + c, x, near1], W1[2 + o, x, pl.ds(7, 24)], zs, zt)
            diagonal = MASS
            for value in values:
                diagonal = diagonal + value
            inverse = 1.0 / diagonal
            D1[c, x] = diagonal
            I1[c, x] = inverse
            for k, value in enumerate(values):
                C1[c, k, x] = value * inverse
        return carry

    lax.fori_loop(2, 14, coefficients1, 0, unroll=2)

    def weighted1(A, c, x):
        o = 1 - c
        pc0 = ((s24 + x + c) & 1) == 0
        here = A[o, x, near1]
        total = B1[c, x, near1] * I1[c, x] + C1[c, 0, x] * A[o, x + 1, near1] + C1[c, 1, x] * A[o, x - 1, near1]
        total = total + C1[c, 2, x] * A[o, x, pl.ds(9, 24)] + C1[c, 3, x] * A[o, x, pl.ds(7, 24)]
        far = jnp.where(pc0, pltpu.roll(here, 1, 1), pltpu.roll(here, LANES - 1, 1))
        return total + C1[c, 4, x] * here + C1[c, 5, x] * far

    def half_sweep1(A, c, low):
        def rows(i, carry):
            x = low + i
            A[c, x, near1] = weighted1(A, c, x)
            return carry

        lax.fori_loop(0, 16 - 2 * low, rows, 0, unroll=8 - low)

    b1_group.wait()

    def first1(x, carry):
        V1[0, x, near1] = B1[0, x, near1] * I1[0, x]
        return carry

    lax.fori_loop(2, 14, first1, 0, unroll=4)
    half_sweep1(V1, 1, 3)
    half_sweep1(V1, 0, 4)
    half_sweep1(V1, 1, 5)

    for i in range(2):
        total = None
        for k in range(2):
            x = 6 + 2 * i + k
            for c in (0, 1):
                r = ((weighted1(V1, c, x) - V1[c, x, near1]) * D1[c, x])[8:16]
                total = r if total is None else total + r
        T1[pl.ds(8, 8), :] = total
        Z[pl.ds(4 * i, 4), :] = (T1[pl.ds(8, 4, stride=2), :] + T1[pl.ds(9, 4, stride=2), :]) * 0.125

    for copy in table_copies:
        copy.wait()
    depth = pl.ds(0, LANES)
    G1[gy] = dot(Z[pl.ds(0, 8), :], STK[depth, :])
    finish = gather(G1, False)
    one = pl.ds(1, 1)
    v1_group = Group()
    v1_group.start(blocks(V1, VB, one) + second(V1, VB, one, ((2, 9, 1), (-2, 6, 14))))
    wait_c2()
    CR[...] = jnp.sum(S2[...], axis=0)
    mean = [jnp.sum(jnp.where(lane == d, CR[...], 0.0), axis=1, keepdims=True) for d in range(3)]
    cells = float(2 * gxn * 4 * gyn * LANES)
    flat_part = MASS + mean[1] * WY[...] + mean[2] * STK[pl.ds(LANES + 8 * gxn, 8), :]

    def eigen(i, carry):
        tile = pl.ds(pl.multiple_of(8 * i, 8), 8)
        DI[tile, :] = 1.0 / ((flat_part + mean[0] * STK[pl.ds(pl.multiple_of(LANES + 8 * i, 8), 8), :]) * cells)
        return carry

    lax.fori_loop(0, gxn, eigen, 0, unroll=4)
    VB[1, pl.ds(6, 4), mine] = V1[1, pl.ds(6, 4), mine]
    VP[1, pl.ds(4, LX), own] = VQ[1, pl.ds(4, LX), own]
    finish()
    G2[gx] = dot(FI[...], G1[...].reshape(8 * gyn, LANES))
    finish = gather(G2, True)
    column_x = (iota((16, 32 * gyn), 1) >> 2) & 7
    for x in range(8):
        M3[pl.ds(16 * x, 16), :] = jnp.where(column_x == x, LT[...], 0.0)
    finish()
    spectrum = dot(AX[pl.ds(0, 8 * gxn), :], G2[...].reshape(8 * gxn, LANES)) * DI[...]
    back_x = dot(AX[pl.ds(pl.multiple_of(8 * gxn + 8 * gx, 8), 32), :], spectrum)
    G3[gy] = dot(back_x, STK[depth, :])
    finish = gather(G3, False)
    v1_group.wait()
    v_group.wait()
    finish()
    coarse = dot(M3[...], G3[...].reshape(32 * gyn, LANES))

    for a in range(8):
        part = coarse[16 * a : 16 * a + 16]
        T1[pl.ds(2, 16, stride=2), :] = part
        T1[pl.ds(3, 16, stride=2), :] = part
        for x in (2 * a, 2 * a + 1):
            VB[1, x, near1] = VB[1, x, near1] + T1[pl.ds(0, 24), :]
    half_sweep1(VB, 0, 2)
    half_sweep1(VB, 1, 3)
    half_sweep1(VB, 0, 4)
    half_sweep1(VB, 1, 5)

    def prolong(i, carry):
        even = ((j12 + i) & 1) == 0
        e, o = VB[0, 4 + i, pl.ds(14, 12)], VB[1, 4 + i, pl.ds(14, 12)]
        for h, part in enumerate((jnp.where(even, e, o), jnp.where(even, o, e))):
            T[i, pl.ds(h, 12, stride=4), :] = part
            T[i, pl.ds(h + 2, 12, stride=4), :] = part
        for x in (2 * i, 2 * i + 1):
            VP[1, x, wide] = VP[1, x, wide] + T[i, pl.ds(0, 48)]
        return carry

    lax.fori_loop(1, 7, prolong, 0, unroll=3)
    half_sweep(VP, 0, VP, True)
    exchanged(VP, 1, V)
    half_sweep(V, 0, V, True)
    half_sweep(V, 1, V, False)

    for x in range(LX):
        even = ((iota((LY, LANES), 0) + x) & 1) == 0
        for h in (0, 1):
            e, o = V[0, x + 4, pl.ds(16 + h, LY, stride=2), :], V[1, x + 4, pl.ds(16 + h, LY, stride=2), :]
            rows = pl.ds(x * LY, LY)
            Q[rows, pl.ds(2 * h * LANES, LANES)] = jnp.where(even, e, o)
            Q[rows, pl.ds((2 * h + 1) * LANES, LANES)] = jnp.where(even, o, e)
    out_ref[...] = permuted(Q[...], pick_ref[...], ((1,), (1,))).reshape(LX, LY, 4 * LANES)


def solution(mesh):
    gxn, gyn = mesh.shape["gx"], mesh.shape["gy"]
    consts = tables(gxn, gyn)

    def step(source, face_coef):
        vmem = pl.BlockSpec(memory_space=pltpu.VMEM)
        dma = pltpu.SemaphoreType.DMA
        V = pltpu.VMEM
        return pl.pallas_call(
            functools.partial(kernel, gxn, gyn),
            out_shape=jax.ShapeDtypeStruct((LX, LY, 4 * LANES), F32),
            in_specs=[vmem] * 2 + [pl.BlockSpec(memory_space=pl.ANY)] * 5 + [vmem],
            out_specs=vmem,
            scratch_shapes=[
                V((8, 16, 64, LANES), F32),
                V((2, 16, 64, LANES), F32),
                V((2, 16, 64, LANES), F32),
                V((2, 16, 64, LANES), F32),
                V((2, 6, 16, 48, LANES), F32),
                V((2, 16, 48, LANES), F32),
                V((2, 16, 48, LANES), F32),
                V((8, 64, LANES), F32),
                V((6, 16, 40, LANES), F32),
                V((2, 16, 24, LANES), F32),
                V((2, 16, 24, LANES), F32),
                V((2, 6, 16, 24, LANES), F32),
                V((2, 16, 40, LANES), F32),
                V((2, 16, 40, LANES), F32),
                V((2, 16, 40, LANES), F32),
                V((48, LANES), F32),
                V((16, LANES), F32),
                V((gyn, 8, LANES), F32),
                V((gxn, 8, LANES), F32),
                V((gyn, 32, LANES), F32),
                V((8 * gxn, LANES), F32),
                V((gyn, 1, LANES), F32),
                V((gxn, 1, LANES), F32),
                V((1, LANES), F32),
                V((LX * LY, 4 * LANES), F32),
                V((16, 32 * gyn), F32),
                V((128, 32 * gyn), F32),
                V((2, 32, LANES), F32),
                V((LANES + 8 * gxn + 8, LANES), F32),
                V((16 * gxn + 24, 8 * gxn), F32),
                V((8, 8 * gyn), F32),
                V((8, LANES), F32),
                V((2048, LANES), F32),
                dma((15,)),
                dma((15,)),
                dma((5,)),
            ],
            compiler_params=pltpu.CompilerParams(
                collective_id=0, has_side_effects=True, vmem_limit_bytes=60 * 1024 * 1024
            ),
            name="cycle",
        )(source, face_coef, *[jnp.asarray(t) for t in consts])

    return jax.shard_map(
        step,
        mesh=mesh,
        in_specs=(P("gx", "gy", None), P(None, "gx", "gy", None)),
        out_specs=P("gx", "gy", None),
        check_vma=False,
    )
```
